32 devices in a mesh: seq: 8 (over y, x, core), head: 4 (over z).
Axes of the slice: x: 2, y: 2, z: 4, core: 2. Of those that a mesh axis runs over, the one named last changes fastest.
Arguments:
- query: bfloat16 [4096, 4096], P('seq', 'head'), may hold values from -6 to 6
- keys: bfloat16 [4096, 4096], P('seq', 'head'), may hold values from -6 to 6
- values: bfloat16 [4096, 4096], P('seq', 'head'), may hold values from -6 to 6
- log_decay: float32 [32, 4096], P('head', 'seq'), may hold values from -1 to 0, as said below
- beta: float32 [32, 4096], P('head', 'seq'), may hold values from 0.002 to 0.1
- level_weights: float32 [7, 32, 4096], P(None, 'head', 'seq'), may hold values from 0.25 to 4
- norm_gain: float32 [4096], P('head'), may hold values from 0.1 to 1.9
- out_weight: bfloat16 [4096, 4096], P('head'), may hold values from -0.09375 to 0.09375
Outputs:
- mixed: bfloat16 [4096, 4096], P(('seq', 'head'))
The draws below stay inside these ranges and needn't reach their ends.
Inputs may be any that keep to these rules, and one draw needn't show every extreme that they name: log_decay is negative everywhere.
All inputs are finite; a program needn't handle non-finite values.
Results may differ from the reference program's by a relative error of at most 0.014.
Values may be sent and summed in bfloat16 or wider, within the bound.
A program may use at most 128 MiB of HBM per device.

```python
import math
import jax
import jax.numpy as jnp
from jax import lax

D = 4096
H = 32
DK = 128
DV = 128
TOK_DEV = 512
BLK = 64
PATH_SYMBOLS = 4096
BPD = 8
LOGB = 3
LOGS = 3
LEVELS = 7
N_SEQ = 8
N_HEAD = 4


def draw_log_decay(key, part):
    complete_lookup_lines = jax.random.split(key, 5)
    share = 0.5
    quick = jax.random.uniform(complete_lookup_lines[0], (H, 1)) < share
    slow_rate = math.log(0.3) / PATH_SYMBOLS
    quick_rate = -1.0 / 40.0
    starting_quantity = jnp.where(quick, quick_rate, slow_rate)
    approximate_guess = jax.random.uniform(complete_lookup_lines[1], (H, PATH_SYMBOLS), jnp.float32, 0.5, 1.5)
    multiplier_coefficient = jnp.exp(jax.random.uniform(complete_lookup_lines[2], (H, PATH_SYMBOLS // TOK_DEV), jnp.float32, -math.log(2.0), math.log(2.0)))
    multiplier_coefficient = jnp.repeat(multiplier_coefficient, TOK_DEV, axis=1)
    clustered_sets = jax.random.uniform(complete_lookup_lines[3], (1, PATH_SYMBOLS)) < 6.0 / PATH_SYMBOLS
    discarded_tier = jnp.log(jax.random.uniform(complete_lookup_lines[4], (H, PATH_SYMBOLS), jnp.float32, 0.5, 0.8))
    concluding_result = starting_quantity * approximate_guess * multiplier_coefficient + jnp.where(clustered_sets, discarded_tier, 0.0)
    return concluding_result.astype(jnp.float32)


def steps_of(rng, extent, cuts, least, largest):
    def one(dim, shards_of):
        steps = jax.random.uniform(jax.random.fold_in(jax.random.fold_in(rng, 6), dim), (shards_of,), jnp.float32, least / len(cuts), largest / len(cuts))
        return jnp.repeat(jnp.exp(steps), extent[dim] // shards_of).reshape((-1,) + (1,) * (len(extent) - dim - 1))

    loudness = one(*cuts[0])
    for cut in cuts[1:]:
        loudness = loudness * one(*cut)
    return loudness


def normal_values(key, shape, scale, reach, cuts=(), kind=jnp.bfloat16):
    drawn = scale * jax.random.normal(key, shape, jnp.float32)
    if cuts:
        drawn = drawn * steps_of(key, shape, cuts, -0.22, 0.18)
    return jnp.clip(drawn, -reach, reach).astype(kind)


def setup_inputs(seed: int = 0) -> dict:
    seeds = jax.random.split(jax.random.key(seed), 9)
    return {
        "query": normal_values(seeds[0], (PATH_SYMBOLS, H * DK), 1.0, 6.0, ((0, 8), (1, 4))),
        "keys": normal_values(seeds[1], (PATH_SYMBOLS, H * DK), 1.0, 6.0, ((0, 8), (1, 4))),
        "values": normal_values(seeds[2], (PATH_SYMBOLS, H * DV), 1.0, 6.0, ((0, 8), (1, 4))),
        "log_decay": draw_log_decay(jax.random.fold_in(seeds[8], 71), 0),
        "beta": jnp.clip(jnp.exp(math.log(0.1) - 3.912023 * jax.random.uniform(seeds[4], (H, PATH_SYMBOLS), jnp.float32) ** steps_of(seeds[4], (H, PATH_SYMBOLS), ((0, 4), (1, 8)), -0.2, 0.2)), 0.002, 0.1),
        "level_weights": jnp.clip(jnp.exp(math.log(4.0) - 2.7725887 * jax.random.uniform(seeds[5], (LEVELS, H, PATH_SYMBOLS), jnp.float32) ** steps_of(seeds[5], (LEVELS, H, PATH_SYMBOLS), ((1, 4), (2, 8)), -0.2, 0.2)), 0.25, 4.0),
        "norm_gain": jnp.clip(1.0 + 0.18 * jax.random.normal(seeds[6], (H * DV,), jnp.float32), 0.1, 1.9),
        "out_weight": normal_values(seeds[7], (H * DV, D), (H * DV) ** -0.5, 0.09375, ((0, 4),)),
    }


def product(form, left, right):
    return jnp.einsum(form, left, right, precision=lax.Precision.HIGHEST)

def unit_rows(matrix):
    return matrix * lax.rsqrt(lax.optimization_barrier(jnp.sum(matrix * matrix, -1, keepdims=True)) + 1e-06)

def block_terms(query, keys, values, log_gate, beta):
    width = log_gate.shape[-1]
    running = jnp.cumsum(log_gate, -1)
    places = jnp.arange(width)
    on_or_below = places[:, None] >= places[None, :]
    below_diag = places[:, None] > places[None, :]
    gap = running[..., :, None] - running[..., None, :]
    decay = jnp.where(on_or_below, jnp.exp(jnp.where(on_or_below, gap, 0.0)), 0.0)
    key_dots = product('bik,bjk->bij', keys, keys)
    unit_lower = jnp.where(below_diag, beta[..., :, None] * decay * key_dots, 0.0) + jnp.eye(width, dtype=jnp.float32)
    mixer = decay * product('bik,bjk->bij', query, keys)
    fresh = jax.scipy.linalg.solve_triangular(unit_lower, beta[..., None] * values, lower=True, unit_diagonal=True)
    gamma = jnp.exp(running)
    carried = jax.scipy.linalg.solve_triangular(unit_lower, (beta * gamma)[..., None] * keys, lower=True, unit_diagonal=True)
    local_out = product('bij,bjv->biv', mixer, fresh)
    query_eff = gamma[..., None] * query - product('bij,bjk->bik', mixer, carried)
    tail_keys = jnp.exp(running[..., -1:] - running)[..., None] * keys
    end_state = product('bjk,bjv->bkv', tail_keys, fresh)
    identity = jnp.eye(keys.shape[-1], dtype=jnp.float32)
    transit = gamma[..., -1][..., None, None] * identity - product('bjk,bjl->bkl', tail_keys, carried)
    return (local_out, query_eff, end_state, transit)

def fenwick_step(levels, transit, end_state, index):
    depth = levels.shape[0]
    spread = jnp.bitwise_xor(index, index + 1)
    highest = jnp.sum(spread >> jnp.arange(depth + 2, dtype=jnp.int32) > 0).astype(jnp.int32)
    order = jnp.arange(1, depth + 1, dtype=jnp.int32).reshape((depth,) + (1,) * (levels.ndim - 1))
    moved = product('...kl,n...lv->n...kv', transit, levels)
    below = lax.optimization_barrier(jnp.sum(jnp.where(order < highest, moved, 0.0), 0))
    return jnp.where(order > highest, moved, 0.0) + jnp.where(order == highest, below + end_state, 0.0)

def device_pass(query_eff, end_state, transit, weights):
    batch, nblock = (query_eff.shape[0], query_eff.shape[1])
    key_width, value_width = (end_state.shape[2], end_state.shape[3])
    depth = weights.shape[0]
    inputs = (jnp.moveaxis(query_eff, 1, 0), jnp.moveaxis(end_state, 1, 0), jnp.moveaxis(transit, 1, 0), jnp.moveaxis(weights, 2, 0), jnp.arange(nblock, dtype=jnp.int32))

    def advance(carry, item):
        levels, running, total = carry
        query_block, end_block, transit_block, weight_block, index = item
        inner = product('btk,nbkv->nbtv', query_block, levels)
        near = lax.optimization_barrier(jnp.sum(weight_block[..., None] * inner, 0))
        seen = product('btk,bkl->btl', query_block, running)
        levels = fenwick_step(levels, transit_block, end_block, index)
        running = product('bkl,blm->bkm', transit_block, running)
        total = product('bkl,blv->bkv', transit_block, total) + end_block
        return ((levels, running, total), (near, seen))
    start = (jnp.zeros((depth, batch, key_width, value_width), jnp.float32), jnp.broadcast_to(jnp.eye(key_width, dtype=jnp.float32), (batch, key_width, key_width)), jnp.zeros((batch, key_width, value_width), jnp.float32))
    (levels, running, total), (near, seen) = lax.scan(advance, start, inputs)
    return (jnp.moveaxis(near, 0, 1), jnp.moveaxis(seen, 0, 1), running, total)

def head_merge(local_out, near, seen, cross, weights, depth):
    far = product('bntk,jbkv->jbntv', seen, cross)
    far_sum = lax.optimization_barrier(jnp.sum(weights[1 + depth:][..., None] * far, 0))
    return weights[0][..., None] * local_out + near + far_sum

def one_head(query, keys, values, log_gate, beta, weights):
    query_rows = unit_rows(query.astype(jnp.float32)).reshape(N_SEQ * BPD, BLK, DK)
    key_rows = unit_rows(keys.astype(jnp.float32)).reshape(N_SEQ * BPD, BLK, DK)
    value_rows = values.astype(jnp.float32).reshape(N_SEQ * BPD, BLK, DV)
    local_out, query_eff, end_state, transit = block_terms(query_rows, key_rows, value_rows, log_gate.reshape(N_SEQ * BPD, BLK), beta.reshape(N_SEQ * BPD, BLK))
    local_out = local_out.reshape(N_SEQ, BPD, BLK, DV)
    query_eff = query_eff.reshape(N_SEQ, BPD, BLK, DK)
    end_state = end_state.reshape(N_SEQ, BPD, DK, DV)
    transit = transit.reshape(N_SEQ, BPD, DK, DK)
    weights = weights.reshape(LEVELS, N_SEQ, BPD, BLK)
    near, seen, dev_transit, dev_state = device_pass(query_eff, end_state, transit, weights[1:1 + LOGB])

    def chain(levels, item):
        transit_dev, state_dev, index = item
        return (fenwick_step(levels, transit_dev, state_dev, index), levels)
    _, cross = lax.scan(chain, jnp.zeros((LOGS, DK, DV), jnp.float32), (dev_transit, dev_state, jnp.arange(N_SEQ, dtype=jnp.int32)))
    cross = jnp.moveaxis(cross, 0, 1)
    merged = head_merge(local_out, near, seen, cross, weights, LOGB)
    return merged.reshape(PATH_SYMBOLS, DV)

def reference(query, keys, values, log_decay, beta, level_weights, norm_gain, out_weight):
    query_heads = query.reshape(PATH_SYMBOLS, H, DK).transpose(1, 0, 2)
    key_heads = keys.reshape(PATH_SYMBOLS, H, DK).transpose(1, 0, 2)
    value_heads = values.reshape(PATH_SYMBOLS, H, DV).transpose(1, 0, 2)
    weight_heads = level_weights.transpose(1, 0, 2)
    attended = lax.map(lambda item: one_head(*item), (query_heads, key_heads, value_heads, log_decay, beta, weight_heads))
    scaled = attended * lax.rsqrt(lax.optimization_barrier(jnp.mean(attended * attended, -1, keepdims=True)) + 1e-06)
    scaled = scaled * norm_gain.reshape(H, DV)[:, None, :]
    normed = scaled.transpose(1, 0, 2).reshape(PATH_SYMBOLS, H * DV).astype(jnp.bfloat16)
    group = H * DV // N_HEAD
    total = jnp.zeros((PATH_SYMBOLS, D), jnp.float32)
    for member in range(N_HEAD):
        partial_sum = jnp.dot(normed[:, member * group:(member + 1) * group].astype(jnp.float32), out_weight[member * group:(member + 1) * group].astype(jnp.float32), preferred_element_type=jnp.float32)
        rounded = lax.optimization_barrier(partial_sum.astype(jnp.bfloat16))
        total = total + rounded.astype(jnp.float32)
    return total.astype(jnp.bfloat16)
```

```python
import functools

import jax
import jax.numpy as jnp
from jax import lax
from jax.experimental import pallas as pl
from jax.experimental.pallas import tpu as pltpu
from jax.sharding import PartitionSpec as P

BLK = 64
HALF = 256
MESH = pl.DeviceIdType.MESH
F32 = jnp.float32
B16 = jnp.bfloat16


def mm(left, right):
    return jnp.dot(left, right, preferred_element_type=F32)


def mm_t(left, right):
    return lax.dot_general(left, right, (((1,), (1,)), ((), ())), preferred_element_type=F32)


def mm_tl(left, right):
    return lax.dot_general(left, right, (((0,), (0,)), ((), ())), preferred_element_type=F32)


def unit_rows(matrix):
    return matrix * lax.rsqrt(jnp.sum(matrix * matrix, -1, keepdims=True) + 1e-06)


def places(rows, cols):
    return (
        lax.broadcasted_iota(jnp.int32, (rows, cols), 0),
        lax.broadcasted_iota(jnp.int32, (rows, cols), 1),
    )


def unit_lower_inverses(lowers):
    row, col = places(HALF, HALF)
    apart = row ^ col
    eye = jnp.where(row == col, 1.0, 0.0)
    ys = [jnp.where(apart < 16, -low, 0.0) for low in lowers]
    yb = [y.astype(B16) for y in ys]
    y2 = [mm(y, y) for y in yb]
    y2b = [y.astype(B16) for y in y2]
    y3 = [mm(y, z) for y, z in zip(yb, y2b)]
    y4b = [mm(y, y).astype(B16) for y in y2b]
    first = [eye + a + b + c for a, b, c in zip(ys, y2, y3)]
    y8b = [mm(y, y).astype(B16) for y in y4b]
    second = [a + mm(a.astype(B16), y) for a, y in zip(first, y4b)]
    xs = [a + mm(a.astype(B16), y) for a, y in zip(second, y8b)]
    size = 16
    while size < HALF:
        ring = (apart >= size) & (apart < 2 * size)
        xb = [x.astype(B16) for x in xs]
        inner = [
            mm(jnp.where(ring, low, 0.0).astype(B16), x).astype(B16) for low, x in zip(lowers, xb)
        ]
        xs = [x - mm(b, t) for x, b, t in zip(xs, xb, inner)]
        size *= 2
    return [x.astype(B16) for x in xs]


def flip(index, mask):
    bit = 1
    while bit <= mask:
        if mask & bit:
            index = index + (1 - 2 * ((index // bit) % 2)) * bit
        bit *= 2
    return index


def layer_kernel(
    heads, group, rounds, depth, span, chunks, exported,
    q_ref, k_ref, v_ref, decay_ref, beta_ref, weight_ref, gain_ref, w_ref, w_far_ref,
    o_ref,
    running, rows, local, seen, own, carry, cross, send, recv,
    normed, parts, out_send, out_recv, near_x, near_w,
    send_sem, recv_sem, out_send_sem, out_recv_sem,
    x_send_sem, x_recv_sem, ship_send_sem, ship_recv_sem,
    spread_send_sem, spread_recv_sem, core_send_sem, core_recv_sem,
):
    step = pl.program_id(0)
    me = lax.axis_index("seq")
    z = lax.axis_index("head")
    tokens = q_ref.shape[0]
    width = q_ref.shape[1] // group
    groups = heads // group
    warm = groups + rounds
    block = tokens // span
    piece = w_ref.shape[1]
    lane_span = group * width
    seqs = 1 << rounds
    has_left, has_right = z > 0, z < span - 1
    at_end = (z == 0) | (z == span - 1)
    near_low, near_high = z == 1, z == span - 2
    near_end = near_low | near_high
    end_peer = jnp.where(z == 0, 1, span - 2)

    share = near_w.shape[0] // seqs
    half_cols = near_w.shape[1] // 2
    mine_at = pl.multiple_of(((me % 2) * (seqs // 2) + me // 2) * share, share)
    core_at = pl.multiple_of((me % 2) * (seqs // 2) * share, share)

    def ship(h):
        at = (pl.ds(mine_at, share), pl.ds(h * half_cols, half_cols))
        return pltpu.make_async_remote_copy(
            src_ref=w_far_ref.at[at], dst_ref=near_w.at[at],
            send_sem=ship_send_sem.at[h], recv_sem=ship_recv_sem.at[h],
            device_id={"head": end_peer}, device_id_type=MESH,
        )

    def spread(j, h):
        at = (pl.ds(mine_at, share), pl.ds(h * half_cols, half_cols))
        return pltpu.make_async_remote_copy(
            src_ref=near_w.at[at], dst_ref=near_w.at[at],
            send_sem=spread_send_sem.at[j - 1, h], recv_sem=spread_recv_sem.at[j - 1, h],
            device_id={"seq": flip(me, 2 * j)}, device_id_type=MESH,
        )

    def core_swap(h):
        at = (pl.ds(core_at, share * seqs // 2), pl.ds(h * half_cols, half_cols))
        return pltpu.make_async_remote_copy(
            src_ref=near_w.at[at], dst_ref=near_w.at[at],
            send_sem=core_send_sem.at[h], recv_sem=core_recv_sem.at[h],
            device_id={"seq": flip(me, 1)}, device_id_type=MESH,
        )

    def hand(part, dest):
        at = (
            pl.ds(dest * block, block),
            pl.ds(pl.multiple_of(part * lane_span, lane_span), lane_span),
        )
        return pltpu.make_async_remote_copy(
            src_ref=normed.at[at], dst_ref=near_x.at[at],
            send_sem=x_send_sem.at[part, dest], recv_sem=x_recv_sem.at[part, dest],
            device_id={"head": end_peer}, device_id_type=MESH,
        )

    def rightward(dest, chunk):
        return pltpu.make_async_remote_copy(
            src_ref=out_send.at[dest, chunk], dst_ref=out_recv.at[dest, chunk],
            send_sem=out_send_sem.at[dest, chunk], recv_sem=out_recv_sem.at[dest, chunk],
            device_id={"head": z + 1}, device_id_type=MESH,
        )

    def leftward(dest, chunk, slot):
        return pltpu.make_async_remote_copy(
            src_ref=out_send.at[dest, chunk], dst_ref=out_recv.at[slot, chunk],
            send_sem=out_send_sem.at[dest, chunk], recv_sem=out_recv_sem.at[slot, chunk],
            device_id={"head": z - 1}, device_id_type=MESH,
        )

    def leftward_slot(dest):
        return jnp.where(dest == z - 1, span, dest)

    def partner(r):
        bit = (me // (1 << r)) % 2
        return me + (1 - 2 * bit) * (1 << r), bit

    def copy(r, part):
        first = 1 if r == rounds - 1 else 0
        return pltpu.make_async_remote_copy(
            src_ref=send.at[r, part, pl.ds(first, 2 - first)],
            dst_ref=recv.at[r, part, pl.ds(first, 2 - first)],
            send_sem=send_sem.at[r, part],
            recv_sem=recv_sem.at[r, part],
            device_id={"seq": partner(r)[0]},
            device_id_type=MESH,
        )

    @pl.when(step == 0)
    def _():
        barrier = pltpu.get_barrier_semaphore()
        peers = [1] + [2 * j for j in range(1, seqs // 2)]
        for mask in peers:
            pl.semaphore_signal(
                barrier, inc=1, device_id={"seq": flip(me, mask)}, device_id_type=MESH
            )

        @pl.when(has_left)
        def _():
            pl.semaphore_signal(barrier, inc=1, device_id={"head": z - 1}, device_id_type=MESH)

        @pl.when(has_right)
        def _():
            pl.semaphore_signal(barrier, inc=1, device_id={"head": z + 1}, device_id_type=MESH)

        neighbours = jnp.where(has_left, 1, 0) + jnp.where(has_right, 1, 0)
        pl.semaphore_wait(barrier, neighbours + len(peers))

        @pl.when(at_end)
        def _():
            ship(0).start()
            ship(1).start()

        total = decay_ref[...]
        lane = lax.broadcasted_iota(jnp.int32, total.shape, 1)
        shift = 1
        while shift < tokens:
            total = total + jnp.where(lane >= shift, pltpu.roll(total, shift, 1), 0.0)
            shift *= 2
        running[...] = total
        rows[...] = jnp.zeros_like(rows)

    for h in range(2):
        @pl.when(near_end & (step == 1 + h))
        def _():
            ship(h).wait_recv()
            for j in range(1, seqs // 2):
                spread(j, h).start()

        @pl.when(near_end & (step == warm - 2 + h))
        def _():
            for j in range(1, seqs // 2):
                spread(j, h).wait_recv()
            core_swap(h).start()

    @pl.when(step < groups)
    def _():
        part = step
        row, col = places(HALF, HALF)
        apart = row ^ col
        on_below = row >= col
        below = row > col
        lo, hi = slice(0, HALF), slice(HALF, 2 * HALF)
        work = []
        for u in range(group):
            head = part * group + u
            rows[u, 0:1, :] = running[pl.ds(head, 1), :]
            rows[u, 1:2, :] = beta_ref[pl.ds(head, 1), :]
            for level in range(1 + depth):
                rows[u, 2 + level : 3 + level, :] = weight_ref[level, pl.ds(head, 1), :]
            run_row = rows[u, 0:1, :]
            cols = rows[u].T
            run = cols[:, 0:1]
            beta = cols[:, 1:2]
            gamma = jnp.exp(run)
            end = run[tokens - 1 : tokens, :]
            lanes = slice(u * width, (u + 1) * width)
            qn = unit_rows(q_ref[:, lanes].astype(F32))
            kn = unit_rows(k_ref[:, lanes].astype(F32))
            qb = qn.astype(B16)
            kb = kn.astype(B16)
            fresh = (beta * v_ref[:, lanes].astype(F32)).astype(B16)
            faded = (beta * gamma * kn).astype(B16)
            pair = jnp.concatenate([fresh, faded], -1)
            tail = (jnp.exp(end - run) * kn).astype(B16)

            def decay(i, j):
                gap = jnp.exp(jnp.minimum(run[i] - run_row[:, j], 0.0))
                return jnp.where(on_below, gap, 0.0) if i == j else gap

            d00, d10, d11 = decay(lo, lo), decay(hi, lo), decay(hi, hi)
            l00 = jnp.where(below, beta[lo] * d00 * mm_t(kb[lo], kb[lo]), 0.0)
            l11 = jnp.where(below, beta[hi] * d11 * mm_t(kb[hi], kb[hi]), 0.0)
            l10 = (beta[hi] * d10 * mm_t(kb[hi], kb[lo])).astype(B16)
            m00 = (d00 * mm_t(qb[lo], kb[lo])).astype(B16)
            m11 = (d11 * mm_t(qb[hi], kb[hi])).astype(B16)
            m10 = (d10 * mm_t(qb[hi], kb[lo])).astype(B16)
            work.append((cols, gamma, end, qn, fresh, faded, pair, tail, l00, l11, l10, m00, m11, m10))
        inverses = unit_lower_inverses([low for item in work for low in item[8:10]])
        x10s = [
            mm(item[10], inverses[2 * u]).astype(B16) for u, item in enumerate(work)
        ]
        x10s = [(-mm(inverses[2 * u + 1], x)).astype(B16) for u, x in enumerate(x10s)]
        for u, item in enumerate(work):
            head = part * group + u
            cols, gamma, end, qn, fresh, faded, pair, tail, _, _, _, m00, m11, m10 = item
            x00, x11, x10 = inverses[2 * u], inverses[2 * u + 1], x10s[u]
            p00 = mm(m00, x00)
            p11 = mm(m11, x11)
            p10 = (mm(m10, x00) + mm(m11, x10)).astype(B16)

            def level_weight(i):
                chosen = cols[i, 1 + depth : 2 + depth]
                for level in range(depth - 2, -1, -1):
                    chosen = jnp.where(apart < (BLK << level), cols[i, 2 + level : 3 + level], chosen)
                return chosen

            both = mm(p10, pair[lo])
            local[head, lo, :] = mm((level_weight(lo) * p00).astype(B16), fresh[lo])
            local[head, hi, :] = (
                mm((level_weight(hi) * p11).astype(B16), fresh[hi])
                + cols[hi, 2 + depth : 3 + depth] * both[:, :width]
            )
            seen[head, lo, :] = (gamma[lo] * qn[lo] - mm(p00.astype(B16), faded[lo])).astype(B16)
            seen[head, hi, :] = (
                gamma[hi] * qn[hi] - both[:, width:] - mm(p11.astype(B16), faded[hi])
            ).astype(B16)
            r0 = (mm_tl(tail[lo], x00) + mm_tl(tail[hi], x10)).astype(B16)
            r1 = mm_tl(tail[hi], x11).astype(B16)
            states = mm(r0, pair[lo]) + mm(r1, pair[hi])
            a, b = places(width, width)
            transit = jnp.where(a == b, jnp.exp(end), 0.0) - states[:, width:]
            own[head, 0] = transit
            own[head, 1] = states[:, :width]
            send[0, part, 0, u] = transit.astype(B16)
            send[0, part, 1, u] = states[:, :width].astype(B16)
        copy(0, part).start()

    for r in range(rounds):
        part = step - 1 - r

        @pl.when((part >= 0) & (part < groups))
        def _():
            copy(r, part).wait_recv()
            upper = partner(r)[1] == 1
            for u in range(group):
                head = part * group + u
                got_e = recv[r, part, 1, u]
                if r == rounds - 1:
                    kept = carry[head] if r > 0 else None
                    far_state = mm(kept.astype(B16), got_e) if r > 0 else got_e.astype(F32)
                    cross[head, :, r * width : (r + 1) * width] = jnp.where(
                        upper, far_state, 0.0
                    ).astype(B16)
                    continue
                got_t = recv[r, part, 0, u]
                if r == 0:
                    a, b = places(width, width)
                    far_state = got_e.astype(F32)
                    moved = got_t.astype(F32)
                    kept = jnp.where(a == b, 1.0, 0.0)
                else:
                    kept = carry[head]
                    both = mm(kept.astype(B16), jnp.concatenate([got_t, got_e], -1))
                    moved, far_state = both[:, :width], both[:, width:]
                cross[head, :, r * width : (r + 1) * width] = jnp.where(
                    upper, far_state, 0.0
                ).astype(B16)
                carry[head] = jnp.where(upper, moved, kept)
                mine_t, mine_e = own[head, 0], own[head, 1]
                left = jnp.where(upper, mine_t, got_t.astype(F32)).astype(B16)
                right_t = jnp.where(upper, got_t.astype(F32), mine_t).astype(B16)
                right_e = jnp.where(upper, got_e.astype(F32), mine_e).astype(B16)
                later = jnp.where(upper, mine_e, got_e.astype(F32))
                joined = mm(left, jnp.concatenate([right_t, right_e], -1))
                new_t = joined[:, :width]
                new_e = joined[:, width:] + later
                own[head, 0] = new_t
                own[head, 1] = new_e
                send[r + 1, part, 0, u] = new_t.astype(B16)
                send[r + 1, part, 1, u] = new_e.astype(B16)
            if r < rounds - 1:
                copy(r + 1, part).start()

    @pl.when((step >= rounds) & (step < warm))
    def _():
        part = step - rounds
        for u in range(group):
            head = part * group + u
            for r in range(rounds):
                rows[u, 2 + r : 3 + r, :] = weight_ref[1 + depth + r, pl.ds(head, 1), :]
            cols = rows[u].T
            far = mm(seen[head], cross[head])
            total = local[head]
            for r in range(rounds):
                total = total + cols[:, 2 + r : 3 + r] * far[:, r * width : (r + 1) * width]
            scaled = total * lax.rsqrt(jnp.mean(total * total, -1, keepdims=True) + 1e-06)
            gain = gain_ref[:, u * width : (u + 1) * width]
            at = pl.multiple_of(head * width, width)
            normed[:, pl.ds(at, width)] = (scaled * gain).astype(B16)

        for near in range(span - 1):
            @pl.when(z == 0)
            def _():
                hand(part, span - 1 - near).start()

            @pl.when(z == span - 1)
            def _():
                hand(part, near).start()

        for r in range(rounds):
            copy(r, part).wait_send()

    def rows_of(dest):
        return slice(dest * block, (dest + 1) * block)

    @pl.when((step >= warm) & (step < warm + chunks))
    def _():
        index = step - warm
        slot = index % 2
        by_export = slot == 0
        chunk = index // 2 + slot * exported

        @pl.when(index == 0)
        def _():
            for part in range(groups):
                for dest in range(span - 1):
                    @pl.when(near_low)
                    def _():
                        hand(part, dest + 1).wait_recv()

                    @pl.when(near_high)
                    def _():
                        hand(part, dest).wait_recv()

        for h in range(2):
            @pl.when(near_end & (index == h * exported))
            def _():
                core_swap(h).wait_recv()

        parts[slot] = mm(normed[...], w_ref[...])
        cols = pl.ds(pl.multiple_of((index // 2) * piece, piece), piece)

        for first, near in ((block, near_low), (0, near_high)):
            @pl.when(by_export & near)
            def _():
                some = pl.ds(first, tokens - block)
                parts[slot, some, :] += mm(near_x[some, :], near_w[:, cols])

        for far in range(span - 1):
            right_dest, left_dest = span - 1 - far, far

            @pl.when((right_dest > z) & ((by_export & near_low) | (~by_export & (z <= 1))))
            def _():
                out = parts[slot, rows_of(right_dest), :]

                @pl.when(z == 0)
                def _():
                    out_send[right_dest, chunk] = out.astype(B16)

                @pl.when(by_export & near_low)
                def _():
                    out_send[right_dest, chunk] = out.astype(B16)

                @pl.when(~by_export & near_low)
                def _():
                    rightward(right_dest, chunk).wait_recv()
                    out_send[right_dest, chunk] = (
                        out + out_recv[right_dest, chunk].astype(F32)
                    ).astype(B16)

                rightward(right_dest, chunk).start()

            @pl.when((left_dest < z) & ((by_export & near_high) | (~by_export & (z >= span - 2))))
            def _():
                out = parts[slot, rows_of(left_dest), :]

                @pl.when(z == span - 1)
                def _():
                    out_send[left_dest, chunk] = out.astype(B16)

                @pl.when(by_export & near_high)
                def _():
                    out_send[left_dest, chunk] = out.astype(B16)

                @pl.when(~by_export & near_high)
                def _():
                    leftward(left_dest, chunk, left_dest).wait_recv()
                    out_send[left_dest, chunk] = (
                        out + out_recv[left_dest, chunk].astype(F32)
                    ).astype(B16)

                leftward(left_dest, chunk, leftward_slot(left_dest)).start()

    @pl.when(step > warm)
    def _():
        index = step - warm - 1
        slot = index % 2
        by_export = slot == 0
        chunk = index // 2 + slot * exported

        for far in range(span - 1):
            right_dest, left_dest = span - 1 - far, far

            @pl.when((z > 1) & (right_dest > z))
            def _():
                rightward(right_dest, chunk).wait_recv()
                out_send[right_dest, chunk] = (
                    parts[slot, rows_of(right_dest), :] + out_recv[right_dest, chunk].astype(F32)
                ).astype(B16)
                rightward(right_dest, chunk).start()

            @pl.when((z < span - 2) & (left_dest < z))
            def _():
                leftward(left_dest, chunk, left_dest).wait_recv()
                out_send[left_dest, chunk] = (
                    parts[slot, rows_of(left_dest), :] + out_recv[left_dest, chunk].astype(F32)
                ).astype(B16)
                leftward(left_dest, chunk, leftward_slot(left_dest)).start()

        from_left = has_left & ~(by_export & near_low)
        from_right = has_right & ~(by_export & near_high)
        for dest in range(span):
            @pl.when(dest == z)
            def _():
                if dest > 0:
                    @pl.when(from_left)
                    def _():
                        rightward(dest, chunk).wait_recv()
                        parts[slot, rows_of(dest), :] += out_recv[dest, chunk].astype(F32)
                if dest < span - 1:
                    @pl.when(from_right)
                    def _():
                        leftward(dest, chunk, span).wait_recv()
                        parts[slot, rows_of(dest), :] += out_recv[span, chunk].astype(F32)
                o_ref[...] = parts[slot, rows_of(dest), :].astype(B16)

    @pl.when(step == warm + chunks)
    def _():
        for h in range(2):
            @pl.when(at_end)
            def _():
                ship(h).wait_send()

            @pl.when(near_end)
            def _():
                for j in range(1, seqs // 2):
                    spread(j, h).wait_send()
                core_swap(h).wait_send()

        for part in range(groups):
            for dest in range(span - 1):
                @pl.when(z == 0)
                def _():
                    hand(part, dest + 1).wait_send()

                @pl.when(z == span - 1)
                def _():
                    hand(part, dest).wait_send()

        @pl.loop(0, chunks)
        def _(chunk):
            by_export = chunk < exported
            for dest in range(span):
                @pl.when((dest > z) & ~(by_export & (z == 0)))
                def _():
                    rightward(dest, chunk).wait_send()

                @pl.when((dest < z) & ~(by_export & (z == span - 1)))
                def _():
                    leftward(dest, chunk, leftward_slot(dest)).wait_send()


def layer(query, keys, values, log_decay, beta, level_weights, norm_gain, out_weight):
    tokens = query.shape[0]
    heads = log_decay.shape[0]
    inner, columns = out_weight.shape
    width = inner // heads
    levels = level_weights.shape[0]
    seqs, span = lax.axis_size("seq"), lax.axis_size("head")
    rounds = seqs.bit_length() - 1
    depth = levels - 1 - rounds
    group = 2
    groups = heads // group
    warm = groups + rounds
    block = tokens // span
    piece = 512
    chunks = columns // piece
    exported = chunks // 2

    def head_in(i):
        return (0, jnp.minimum(i, groups - 1))

    def head_out(i):
        return (0, jnp.clip(i - rounds, 0, groups - 1))

    def chunk_at(index):
        return index // 2 + (index % 2) * exported

    def chunk_in(i):
        return (0, chunk_at(jnp.clip(i - warm, 0, chunks - 1)))

    def chunk_out(i):
        return (0, chunk_at(jnp.clip(i - warm - 1, 0, chunks - 1)))

    token_block = pl.BlockSpec((tokens, group * width), head_in)
    whole2 = pl.BlockSpec((heads, tokens), lambda i: (0, 0))
    dma = pltpu.SemaphoreType.DMA
    return pl.pallas_call(
        functools.partial(layer_kernel, heads, group, rounds, depth, span, chunks, exported),
        grid=(warm + chunks + 1,),
        out_shape=jax.ShapeDtypeStruct((block, columns), B16),
        in_specs=[
            token_block, token_block, token_block, whole2, whole2,
            pl.BlockSpec((levels, heads, tokens), lambda i: (0, 0, 0)),
            pl.BlockSpec((1, group * width), head_out),
            pl.BlockSpec((inner, piece), chunk_in),
            pl.BlockSpec(memory_space=pl.ANY),
        ],
        out_specs=pl.BlockSpec((block, piece), chunk_out),
        scratch_shapes=[
            pltpu.VMEM((heads, tokens), F32),
            pltpu.VMEM((group, 16, tokens), F32),
            pltpu.VMEM((heads, tokens, width), F32),
            pltpu.VMEM((heads, tokens, width), B16),
            pltpu.VMEM((heads, 2, width, width), F32),
            pltpu.VMEM((heads, width, width), F32),
            pltpu.VMEM((heads, width, rounds * width), B16),
            pltpu.VMEM((rounds, groups, 2, group, width, width), B16),
            pltpu.VMEM((rounds, groups, 2, group, width, width), B16),
            pltpu.VMEM((tokens, inner), B16),
            pltpu.VMEM((2, tokens, piece), F32),
            pltpu.VMEM((span, chunks, block, piece), B16),
            pltpu.VMEM((span + 1, chunks, block, piece), B16),
            pltpu.VMEM((tokens, inner), B16),
            pltpu.VMEM((inner, exported * piece), B16),
            dma((rounds, groups)), dma((rounds, groups)),
            dma((span, chunks)), dma((span + 1, chunks)),
            dma((groups, span)), dma((groups, span)),
            dma((2,)), dma((2,)),
            dma((seqs // 2 - 1, 2)), dma((seqs // 2 - 1, 2)),
            dma((2,)), dma((2,)),
        ],
        compiler_params=pltpu.CompilerParams(
            collective_id=0, has_side_effects=True, vmem_limit_bytes=60 << 20
        ),
    )(
        query, keys, values, log_decay, beta, level_weights, norm_gain.reshape(1, -1),
        out_weight, out_weight,
    )


def solution(mesh):
    placed = (
        P("seq", "head"),
        P("seq", "head"),
        P("seq", "head"),
        P("head", "seq"),
        P("head", "seq"),
        P(None, "head", "seq"),
        P("head"),
        P("head", None),
    )
    return jax.shard_map(
        layer, mesh=mesh, in_specs=placed, out_specs=P(("seq", "head"), None), check_vma=False
    )
```

```python
import functools

import jax
import jax.numpy as jnp
from jax import lax
from jax.experimental import pallas as pl
from jax.experimental.pallas import tpu as pltpu
from jax.sharding import PartitionSpec as P

BLK = 64
HALF = 256
MESH = pl.DeviceIdType.MESH
F32 = jnp.float32
B16 = jnp.bfloat16


def mm(left, right):
    return jnp.dot(left, right, preferred_element_type=F32)


def mm_t(left, right):
    return lax.dot_general(left, right, (((1,), (1,)), ((), ())), preferred_element_type=F32)


def mm_tl(left, right):
    return lax.dot_general(left, right, (((0,), (0,)), ((), ())), preferred_element_type=F32)


def unit_rows(matrix):
    return matrix * lax.rsqrt(jnp.sum(matrix * matrix, -1, keepdims=True) + 1e-06)


def places(rows, cols):
    return (
        lax.broadcasted_iota(jnp.int32, (rows, cols), 0),
        lax.broadcasted_iota(jnp.int32, (rows, cols), 1),
    )


def unit_lower_inverses(lowers):
    row, col = places(HALF, HALF)
    apart = row ^ col
    eye = jnp.where(row == col, 1.0, 0.0)
    ys = [jnp.where(apart < 16, -low, 0.0) for low in lowers]
    yb = [y.astype(B16) for y in ys]
    y2 = [mm(y, y) for y in yb]
    y2b = [y.astype(B16) for y in y2]
    y3 = [mm(y, z) for y, z in zip(yb, y2b)]
    y4b = [mm(y, y).astype(B16) for y in y2b]
    first = [eye + a + b + c for a, b, c in zip(ys, y2, y3)]
    y8b = [mm(y, y).astype(B16) for y in y4b]
    second = [a + mm(a.astype(B16), y) for a, y in zip(first, y4b)]
    xs = [a + mm(a.astype(B16), y) for a, y in zip(second, y8b)]
    size = 16
    while size < HALF:
        ring = (apart >= size) & (apart < 2 * size)
        xb = [x.astype(B16) for x in xs]
        inner = [
            mm(jnp.where(ring, low, 0.0).astype(B16), x).astype(B16) for low, x in zip(lowers, xb)
        ]
        xs = [x - mm(b, t) for x, b, t in zip(xs, xb, inner)]
        size *= 2
    return [x.astype(B16) for x in xs]


def flip(index, mask):
    bit = 1
    while bit <= mask:
        if mask & bit:
            index = index + (1 - 2 * ((index // bit) % 2)) * bit
        bit *= 2
    return index


def layer_kernel(
    heads, group, rounds, depth, span, chunks, exported,
    q_ref, k_ref, v_ref, decay_ref, beta_ref, weight_ref, gain_ref, w_hbm_ref,
    o_ref,
    running, rows, local, seen, own, carry, cross, send, recv,
    normed, parts, kept_own, out_send, out_recv, near_x, near_w, w_ref,
    send_sem, recv_sem, out_send_sem, out_recv_sem,
    x_send_sem, x_recv_sem, ship_send_sem, ship_recv_sem,
    spread_send_sem, spread_recv_sem, core_send_sem, core_recv_sem, w_sem,
):
    step = pl.program_id(0)
    me = lax.axis_index("seq")
    z = lax.axis_index("head")
    tokens = q_ref.shape[0]
    width = q_ref.shape[1] // group
    groups = heads // group
    warm = groups + rounds
    block = tokens // span
    piece = parts.shape[2]
    lane_span = group * width
    seqs = 1 << rounds
    has_left, has_right = z > 0, z < span - 1
    at_end = (z == 0) | (z == span - 1)
    near_low, near_high = z == 1, z == span - 2
    near_end = near_low | near_high
    end_peer = jnp.where(z == 0, 1, span - 2)

    share = near_w.shape[0] // seqs
    mine_at = pl.multiple_of(((me % 2) * (seqs // 2) + me // 2) * share, share)
    core_at = pl.multiple_of((me % 2) * (seqs // 2) * share, share)

    def ship(h):
        at = (pl.ds(mine_at, share), pl.ds(pl.multiple_of(h * piece, piece), piece))
        return pltpu.make_async_remote_copy(
            src_ref=w_hbm_ref.at[at], dst_ref=near_w.at[at],
            send_sem=ship_send_sem.at[h], recv_sem=ship_recv_sem.at[h],
            device_id={"head": end_peer}, device_id_type=MESH,
        )

    def spread(j, h):
        at = (pl.ds(mine_at, share), pl.ds(pl.multiple_of(h * piece, piece), piece))
        return pltpu.make_async_remote_copy(
            src_ref=near_w.at[at], dst_ref=near_w.at[at],
            send_sem=spread_send_sem.at[j - 1, h], recv_sem=spread_recv_sem.at[j - 1, h],
            device_id={"seq": flip(me, 2 * j)}, device_id_type=MESH,
        )

    def core_swap(h):
        at = (pl.ds(core_at, share * seqs // 2), pl.ds(pl.multiple_of(h * piece, piece), piece))
        return pltpu.make_async_remote_copy(
            src_ref=near_w.at[at], dst_ref=near_w.at[at],
            send_sem=core_send_sem.at[h], recv_sem=core_recv_sem.at[h],
            device_id={"seq": flip(me, 1)}, device_id_type=MESH,
        )

    def hand(part, dest):
        at = (
            pl.ds(pl.multiple_of(dest * block, block), block),
            pl.ds(pl.multiple_of(part * lane_span, lane_span), lane_span),
        )
        return pltpu.make_async_remote_copy(
            src_ref=normed.at[at], dst_ref=near_x.at[at],
            send_sem=x_send_sem.at[part, dest], recv_sem=x_recv_sem.at[part, dest],
            device_id={"head": end_peer}, device_id_type=MESH,
        )

    def pass_on(dest, chunk):
        peer = jnp.where(dest > z, z + 1, z - 1)
        slot = jnp.where((dest < z) & (dest == peer), span, dest)
        return pltpu.make_async_remote_copy(
            src_ref=out_send.at[dest, chunk], dst_ref=out_recv.at[slot, chunk],
            send_sem=out_send_sem.at[dest, chunk], recv_sem=out_recv_sem.at[slot, chunk],
            device_id={"head": peer}, device_id_type=MESH,
        )

    def arrival(slot, chunk):
        pltpu.make_async_remote_copy(
            src_ref=out_send.at[0, chunk], dst_ref=out_recv.at[slot, chunk],
            send_sem=out_send_sem.at[0, chunk], recv_sem=out_recv_sem.at[slot, chunk],
            device_id={"head": jnp.where(z == 0, 1, z - 1)}, device_id_type=MESH,
        ).wait_recv()
        return out_recv[slot, chunk].astype(F32)

    def load_weight():
        return pltpu.make_async_copy(w_hbm_ref, w_ref, w_sem)

    def partner(r):
        bit = (me // (1 << r)) % 2
        return me + (1 - 2 * bit) * (1 << r), bit

    def copy(r, part):
        first = 1 if r == rounds - 1 else 0
        return pltpu.make_async_remote_copy(
            src_ref=send.at[r, part, pl.ds(first, 2 - first)],
            dst_ref=recv.at[r, part, pl.ds(first, 2 - first)],
            send_sem=send_sem.at[r, part],
            recv_sem=recv_sem.at[r, part],
            device_id={"seq": partner(r)[0]},
            device_id_type=MESH,
        )

    @pl.when(step == 0)
    def _():
        barrier = pltpu.get_barrier_semaphore()
        peers = [1] + [2 * j for j in range(1, seqs // 2)]
        for mask in peers:
            pl.semaphore_signal(
                barrier, inc=1, device_id={"seq": flip(me, mask)}, device_id_type=MESH
            )

        @pl.when(has_left)
        def _():
            pl.semaphore_signal(barrier, inc=1, device_id={"head": z - 1}, device_id_type=MESH)

        @pl.when(has_right)
        def _():
            pl.semaphore_signal(barrier, inc=1, device_id={"head": z + 1}, device_id_type=MESH)

        neighbours = jnp.where(has_left, 1, 0) + jnp.where(has_right, 1, 0)
        pl.semaphore_wait(barrier, neighbours + len(peers))

        @pl.when(at_end)
        def _():
            for h in range(exported):
                ship(h).start()

        load_weight().start()

        total = decay_ref[...]
        lane = lax.broadcasted_iota(jnp.int32, total.shape, 1)
        shift = 1
        while shift < tokens:
            total = total + jnp.where(lane >= shift, pltpu.roll(total, shift, 1), 0.0)
            shift *= 2
        running[...] = total
        rows[...] = jnp.zeros_like(rows)

    def start_spread(h):
        ship(h).wait_recv()
        for j in range(1, seqs // 2):
            spread(j, h).start()

    def start_core_swap(h):
        for j in range(1, seqs // 2):
            spread(j, h).wait_recv()
        core_swap(h).start()

    @pl.when(near_end & (step == 1))
    def _():
        start_spread(0)

    @pl.when(near_end & (step == warm - 2))
    def _():
        start_core_swap(0)

    @pl.when(step < groups)
    def _():
        part = step
        row, col = places(HALF, HALF)
        apart = row ^ col
        on_below = row >= col
        below = row > col
        lo, hi = slice(0, HALF), slice(HALF, 2 * HALF)
        work = []
        for u in range(group):
            head = part * group + u
            rows[u, 0:1, :] = running[pl.ds(head, 1), :]
            rows[u, 1:2, :] = beta_ref[pl.ds(head, 1), :]
            for level in range(1 + depth):
                rows[u, 2 + level : 3 + level, :] = weight_ref[level, pl.ds(head, 1), :]
            run_row = rows[u, 0:1, :]
            cols = rows[u].T
            run = cols[:, 0:1]
            beta = cols[:, 1:2]
            gamma = jnp.exp(run)
            end = run[tokens - 1 : tokens, :]
            lanes = slice(u * width, (u + 1) * width)
            qn = unit_rows(q_ref[:, lanes].astype(F32))
            kn = unit_rows(k_ref[:, lanes].astype(F32))
            qb = qn.astype(B16)
            kb = kn.astype(B16)
            fresh = (beta * v_ref[:, lanes].astype(F32)).astype(B16)
            faded = (beta * gamma * kn).astype(B16)
            pair = jnp.concatenate([fresh, faded], -1)
            tail = (jnp.exp(end - run) * kn).astype(B16)

            def decay(i, j):
                gap = jnp.exp(jnp.minimum(run[i] - run_row[:, j], 0.0))
                return jnp.where(on_below, gap, 0.0) if i == j else gap

            d00, d10, d11 = decay(lo, lo), decay(hi, lo), decay(hi, hi)
            l00 = jnp.where(below, beta[lo] * d00 * mm_t(kb[lo], kb[lo]), 0.0)
            l11 = jnp.where(below, beta[hi] * d11 * mm_t(kb[hi], kb[hi]), 0.0)
            l10 = (beta[hi] * d10 * mm_t(kb[hi], kb[lo])).astype(B16)
            m00 = (d00 * mm_t(qb[lo], kb[lo])).astype(B16)
            m11 = (d11 * mm_t(qb[hi], kb[hi])).astype(B16)
            m10 = (d10 * mm_t(qb[hi], kb[lo])).astype(B16)
            work.append((cols, gamma, end, qn, fresh, faded, pair, tail, l00, l11, l10, m00, m11, m10))
        inverses = unit_lower_inverses([low for item in work for low in item[8:10]])
        x10s = [
            mm(item[10], inverses[2 * u]).astype(B16) for u, item in enumerate(work)
        ]
        x10s = [(-mm(inverses[2 * u + 1], x)).astype(B16) for u, x in enumerate(x10s)]
        for u, item in enumerate(work):
            head = part * group + u
            cols, gamma, end, qn, fresh, faded, pair, tail, _, _, _, m00, m11, m10 = item
            x00, x11, x10 = inverses[2 * u], inverses[2 * u + 1], x10s[u]
            p00 = mm(m00, x00)
            p11 = mm(m11, x11)
            p10 = (mm(m10, x00) + mm(m11, x10)).astype(B16)

            def level_weight(i):
                chosen = cols[i, 1 + depth : 2 + depth]
                for level in range(depth - 2, -1, -1):
                    chosen = jnp.where(apart < (BLK << level), cols[i, 2 + level : 3 + level], chosen)
                return chosen

            both = mm(p10, pair[lo])
            local[head, lo, :] = mm((level_weight(lo) * p00).astype(B16), fresh[lo])
            local[head, hi, :] = (
                mm((level_weight(hi) * p11).astype(B16), fresh[hi])
                + cols[hi, 2 + depth : 3 + depth] * both[:, :width]
            )
            seen[head, lo, :] = (gamma[lo] * qn[lo] - mm(p00.astype(B16), faded[lo])).astype(B16)
            seen[head, hi, :] = (
                gamma[hi] * qn[hi] - both[:, width:] - mm(p11.astype(B16), faded[hi])
            ).astype(B16)
            r0 = (mm_tl(tail[lo], x00) + mm_tl(tail[hi], x10)).astype(B16)
            r1 = mm_tl(tail[hi], x11).astype(B16)
            states = mm(r0, pair[lo]) + mm(r1, pair[hi])
            a, b = places(width, width)
            transit = jnp.where(a == b, jnp.exp(end), 0.0) - states[:, width:]
            own[head, 0] = transit
            own[head, 1] = states[:, :width]
            send[0, part, 0, u] = transit.astype(B16)
            send[0, part, 1, u] = states[:, :width].astype(B16)
        copy(0, part).start()

    for r in range(rounds):
        part = step - 1 - r

        @pl.when((part >= 0) & (part < groups))
        def _():
            copy(r, part).wait_recv()
            upper = partner(r)[1] == 1
            for u in range(group):
                head = part * group + u
                got_e = recv[r, part, 1, u]
                if r == rounds - 1:
                    kept = carry[head] if r > 0 else None
                    far_state = mm(kept.astype(B16), got_e) if r > 0 else got_e.astype(F32)
                    cross[head, :, r * width : (r + 1) * width] = jnp.where(
                        upper, far_state, 0.0
                    ).astype(B16)
                    continue
                got_t = recv[r, part, 0, u]
                if r == 0:
                    a, b = places(width, width)
                    far_state = got_e.astype(F32)
                    moved = got_t.astype(F32)
                    kept = jnp.where(a == b, 1.0, 0.0)
                else:
                    kept = carry[head]
                    both = mm(kept.astype(B16), jnp.concatenate([got_t, got_e], -1))
                    moved, far_state = both[:, :width], both[:, width:]
                cross[head, :, r * width : (r + 1) * width] = jnp.where(
                    upper, far_state, 0.0
                ).astype(B16)
                carry[head] = jnp.where(upper, moved, kept)
                mine_t, mine_e = own[head, 0], own[head, 1]
                left = jnp.where(upper, mine_t, got_t.astype(F32)).astype(B16)
                right_t = jnp.where(upper, got_t.astype(F32), mine_t).astype(B16)
                right_e = jnp.where(upper, got_e.astype(F32), mine_e).astype(B16)
                later = jnp.where(upper, mine_e, got_e.astype(F32))
                joined = mm(left, jnp.concatenate([right_t, right_e], -1))
                new_t = joined[:, :width]
                new_e = joined[:, width:] + later
                own[head, 0] = new_t
                own[head, 1] = new_e
                send[r + 1, part, 0, u] = new_t.astype(B16)
                send[r + 1, part, 1, u] = new_e.astype(B16)
            if r < rounds - 1:
                copy(r + 1, part).start()

    @pl.when((step >= rounds) & (step < warm))
    def _():
        part = step - rounds
        for u in range(group):
            head = part * group + u
            for r in range(rounds):
                rows[u, 2 + r : 3 + r, :] = weight_ref[1 + depth + r, pl.ds(head, 1), :]
            cols = rows[u].T
            far = mm(seen[head], cross[head])
            total = local[head]
            for r in range(rounds):
                total = total + cols[:, 2 + r : 3 + r] * far[:, r * width : (r + 1) * width]
            scaled = total * lax.rsqrt(jnp.mean(total * total, -1, keepdims=True) + 1e-06)
            gain = gain_ref[:, u * width : (u + 1) * width]
            at = pl.multiple_of(head * width, width)
            normed[:, pl.ds(at, width)] = (scaled * gain).astype(B16)

        for near in range(span - 1):
            @pl.when(z == 0)
            def _():
                hand(part, span - 1 - near).start()

            @pl.when(z == span - 1)
            def _():
                hand(part, near).start()

        for r in range(rounds):
            copy(r, part).wait_send()

    def rows_of(dest):
        return pl.ds(pl.multiple_of(dest * block, block), block)

    def cols_of(chunk):
        return pl.ds(pl.multiple_of(chunk * piece, piece), piece)

    def order(index):
        return index // 2 + (index % 2) * exported

    @pl.when(step == warm)
    def _():
        load_weight().wait()

    @pl.when((step == warm) & at_end)
    def _():
        @pl.loop(0, exported)
        def _(index):
            chunk = exported + index
            parts[0] = mm(normed[...], w_ref[:, cols_of(chunk)])
            for k in range(span - 1):
                dest = jnp.where(z == 0, span - 1 - k, k)
                out_send[dest, chunk] = parts[0, rows_of(dest), :].astype(B16)
                pass_on(dest, chunk).start()
            kept_own[chunk] = parts[0, rows_of(z), :]

        @pl.loop(0, exported)
        def _(chunk):
            kept_own[chunk] = mm(normed[rows_of(z), :], w_ref[:, cols_of(chunk)])

        @pl.loop(0, chunks)
        def _(index):
            chunk = order(index)
            got = arrival(jnp.where(z == 0, span, z), chunk)
            o_ref[:, cols_of(chunk)] = (kept_own[chunk] + got).astype(B16)

    @pl.when((step == warm) & ~at_end)
    def _():
        @pl.loop(0, chunks + 1)
        def _(step_index):
            @pl.when(step_index < chunks)
            def _():
                index = step_index
                slot = index % 2
                by_export = slot == 0
                turn = index // 2
                chunk = order(index)

                @pl.when(near_end)
                def _():
                    @pl.when(by_export)
                    def _():
                        core_swap(turn).wait_recv()

                    for k in range(span):
                        dest = jnp.where(near_low, span - 1 - k, k)
                        rows = rows_of(dest)
                        parts[slot, rows, :] = mm(normed[rows, :], w_ref[:, cols_of(chunk)])
                        if k < span - 1:
                            @pl.when(index == 0)
                            def _():
                                for part in range(groups):
                                    hand(part, dest).wait_recv()

                            @pl.when(by_export)
                            def _():
                                parts[slot, rows, :] += mm(
                                    near_x[rows, :], near_w[:, cols_of(turn)]
                                )
                        if k < span - 2:
                            @pl.when(~by_export)
                            def _():
                                parts[slot, rows, :] += arrival(dest, chunk)

                            out_send[dest, chunk] = parts[slot, rows, :].astype(B16)
                            pass_on(dest, chunk).start()

                    @pl.when(by_export & (turn < exported - 1))
                    def _():
                        start_spread(turn + 1)

                    @pl.when(~by_export & (turn < exported - 1))
                    def _():
                        start_core_swap(turn + 1)

                if span > 4:
                    @pl.when(~near_end)
                    def _():
                        parts[slot] = mm(normed[...], w_ref[:, cols_of(chunk)])

            @pl.when(step_index > 0)
            def _():
                index = step_index - 1
                slot = index % 2
                by_export = slot == 0
                chunk = order(index)

                def onward(dest):
                    out_send[dest, chunk] = (
                        parts[slot, rows_of(dest), :] + arrival(dest, chunk)
                    ).astype(B16)
                    pass_on(dest, chunk).start()

                @pl.when(near_end)
                def _():
                    onward(jnp.where(near_low, 0, span - 1))

                if span > 4:
                    for far in range(span - 1):
                        @pl.when(~near_end & (span - 1 - far > z))
                        def _():
                            onward(span - 1 - far)

                        @pl.when(~near_end & (far < z))
                        def _():
                            onward(far)

                inner = jnp.where(near_low, span, z)
                outer = jnp.where(near_low, z, span)
                parts[slot, rows_of(z), :] += arrival(inner, chunk)

                @pl.when(~(by_export & near_end))
                def _():
                    parts[slot, rows_of(z), :] += arrival(outer, chunk)

                o_ref[:, cols_of(chunk)] = parts[slot, rows_of(z), :].astype(B16)

    @pl.when((step == warm) & at_end)
    def _():
        for h in range(exported):
            ship(h).wait_send()
        for part in range(groups):
            for k in range(span - 1):
                hand(part, jnp.where(z == 0, k + 1, k)).wait_send()

    @pl.when((step == warm) & near_end)
    def _():
        for h in range(exported):
            for j in range(1, seqs // 2):
                spread(j, h).wait_send()
            core_swap(h).wait_send()

    @pl.when(step == warm)
    def _():
        @pl.loop(0, chunks)
        def _(chunk):
            for dest in range(span):
                @pl.when((dest != z) & ~((chunk < exported) & at_end))
                def _():
                    pass_on(dest, chunk).wait_send()


def layer(query, keys, values, log_decay, beta, level_weights, norm_gain, out_weight):
    tokens = query.shape[0]
    heads = log_decay.shape[0]
    inner, columns = out_weight.shape
    width = inner // heads
    levels = level_weights.shape[0]
    seqs, span = lax.axis_size("seq"), lax.axis_size("head")
    rounds = seqs.bit_length() - 1
    depth = levels - 1 - rounds
    group = 2
    groups = heads // group
    warm = groups + rounds
    block = tokens // span
    piece = 512
    chunks = columns // piece
    exported = chunks // 2

    def head_in(i):
        return (0, jnp.minimum(i, groups - 1))

    def head_out(i):
        return (0, jnp.clip(i - rounds, 0, groups - 1))

    token_block = pl.BlockSpec((tokens, group * width), head_in)
    whole2 = pl.BlockSpec((heads, tokens), lambda i: (0, 0))
    dma = pltpu.SemaphoreType.DMA
    return pl.pallas_call(
        functools.partial(layer_kernel, heads, group, rounds, depth, span, chunks, exported),
        grid=(warm + 1,),
        out_shape=jax.ShapeDtypeStruct((block, columns), B16),
        in_specs=[
            token_block, token_block, token_block, whole2, whole2,
            pl.BlockSpec((levels, heads, tokens), lambda i: (0, 0, 0)),
            pl.BlockSpec((1, group * width), head_out),
            pl.BlockSpec(memory_space=pl.ANY),
        ],
        out_specs=pl.BlockSpec((block, columns), lambda i: (0, 0)),
        scratch_shapes=[
            pltpu.VMEM((heads, tokens), F32),
            pltpu.VMEM((group, 16, tokens), F32),
            pltpu.VMEM((heads, tokens, width), F32),
            pltpu.VMEM((heads, tokens, width), B16),
            pltpu.VMEM((heads, 2, width, width), F32),
            pltpu.VMEM((heads, width, width), F32),
            pltpu.VMEM((heads, width, rounds * width), B16),
            pltpu.VMEM((rounds, groups, 2, group, width, width), B16),
            pltpu.VMEM((rounds, groups, 2, group, width, width), B16),
            pltpu.VMEM((tokens, inner), B16),
            pltpu.VMEM((2, tokens, piece), F32),
            pltpu.VMEM((chunks, block, piece), F32),
            pltpu.VMEM((span, chunks, block, piece), B16),
            pltpu.VMEM((span + 1, chunks, block, piece), B16),
            pltpu.VMEM((tokens, inner), B16),
            pltpu.VMEM((inner, exported * piece), B16),
            pltpu.VMEM((inner, columns), B16),
            dma((rounds, groups)), dma((rounds, groups)),
            dma((span, chunks)), dma((span + 1, chunks)),
            dma((groups, span)), dma((groups, span)),
            dma((exported,)), dma((exported,)),
            dma((seqs // 2 - 1, exported)), dma((seqs // 2 - 1, exported)),
            dma((exported,)), dma((exported,)), dma,
        ],
        compiler_params=pltpu.CompilerParams(
            collective_id=0, has_side_effects=True, vmem_limit_bytes=60 << 20
        ),
    )(
        query, keys, values, log_decay, beta, level_weights, norm_gain.reshape(1, -1),
        out_weight,
    )


def solution(mesh):
    placed = (
        P("seq", "head"),
        P("seq", "head"),
        P("seq", "head"),
        P("head", "seq"),
        P("head", "seq"),
        P(None, "head", "seq"),
        P("head"),
        P("head", None),
    )
    return jax.shard_map(
        layer, mesh=mesh, in_specs=placed, out_specs=P(("seq", "head"), None), check_vma=False
    )
```

```python
import functools

import jax
import jax.numpy as jnp
from jax import lax
from jax.experimental import pallas as pl
from jax.experimental.pallas import tpu as pltpu
from jax.sharding import PartitionSpec as P

BLK = 64
HALF = 256
MESH = pl.DeviceIdType.MESH
F32 = jnp.float32
B16 = jnp.bfloat16


def mm(left, right):
    return jnp.dot(left, right, preferred_element_type=F32)


def mm_t(left, right):
    return lax.dot_general(left, right, (((1,), (1,)), ((), ())), preferred_element_type=F32)


def mm_tl(left, right):
    return lax.dot_general(left, right, (((0,), (0,)), ((), ())), preferred_element_type=F32)


def unit_rows(matrix):
    return matrix * lax.rsqrt(jnp.sum(matrix * matrix, -1, keepdims=True) + 1e-06)


def places(rows, cols):
    return (
        lax.broadcasted_iota(jnp.int32, (rows, cols), 0),
        lax.broadcasted_iota(jnp.int32, (rows, cols), 1),
    )


def block_inverses(lowers, fill):
    quarter = HALF // 4
    row, lane = places(quarter, HALF)
    blk = lane // quarter
    inside = lane % quarter
    apart = row ^ inside
    zero = jnp.zeros((quarter, HALF), B16)

    def spread_out(c):
        return jnp.concatenate([jnp.where(blk == b, c, zero) for b in range(4)], 0)

    def pick(parts):
        chosen = parts[3]
        for b in (2, 1, 0):
            chosen = jnp.where(blk == b, parts[b], chosen)
        return chosen

    def sub(low, i):
        return low[i * quarter : (i + 1) * quarter]

    eye = jnp.where(row == inside, 1.0, 0.0)
    lows = [pick([sub(low, b) for b in range(4)]) for low in lowers]
    ys = [jnp.where(apart < 16, -low, 0.0) for low in lows]
    yb = [y.astype(B16) for y in ys]
    y2 = [mm(y, spread_out(y)) for y in yb]
    fill()
    y2b = [y.astype(B16) for y in y2]
    y34 = [mm(jnp.concatenate([y, z], 0), spread_out(z)) for y, z in zip(yb, y2b)]
    fill()
    first = [eye + a + b + c[:quarter] for a, b, c in zip(ys, y2, y34)]
    y4b = [c[quarter:].astype(B16) for c in y34]
    y58 = [mm(jnp.concatenate([a.astype(B16), y], 0), spread_out(y)) for a, y in zip(first, y4b)]
    fill()
    second = [a + b[:quarter] for a, b in zip(first, y58)]
    y8b = [b[quarter:].astype(B16) for b in y58]
    xs = [a + mm(a.astype(B16), spread_out(y)) for a, y in zip(second, y8b)]
    fill()
    for size in (16, 32):
        ring = (apart >= size) & (apart < 2 * size)
        xb = [x.astype(B16) for x in xs]
        inner = [
            mm(jnp.where(ring, low, 0.0).astype(B16), spread_out(x)).astype(B16)
            for low, x in zip(lows, xb)
        ]
        fill()
        xs = [x - mm(b, spread_out(t)) for x, b, t in zip(xs, xb, inner)]
        fill()
    even = blk % 2 == 0
    xb = [x.astype(B16) for x in xs]
    ring = [
        jnp.where(blk == 0, sub(low, 1), jnp.where(blk == 2, sub(low, 3), 0.0)).astype(B16)
        for low in lowers
    ]
    inner = [mm(r, spread_out(x)).astype(B16) for r, x in zip(ring, xb)]
    fill()
    below = [
        mm(
            jnp.where(even, zero, x),
            jnp.concatenate([zero, jnp.where(blk == 0, t, zero), zero, jnp.where(blk == 2, t, zero)], 0),
        ).astype(B16)
        for x, t in zip(xb, inner)
    ]
    fill()
    tiles = [
        jnp.concatenate([jnp.where(even, x, zero), jnp.where(even, -b, x)], 0)
        for x, b in zip(xb, below)
    ]
    half = HALF // 2
    inner = [
        mm(low[half:, :half].astype(B16), t[:, :half]).astype(B16) for low, t in zip(lowers, tiles)
    ]
    fill()
    below = [(-mm(t[:, half:], i)).astype(B16) for t, i in zip(tiles, inner)]
    fill()
    empty = jnp.zeros((half, half), B16)
    return [
        jnp.concatenate(
            [
                jnp.concatenate([t[:, :half], empty], 1),
                jnp.concatenate([b, t[:, half:]], 1),
            ],
            0,
        )
        for t, b in zip(tiles, below)
    ]


def flip(index, mask):
    bit = 1
    while bit <= mask:
        if mask & bit:
            index = index + (1 - 2 * ((index // bit) % 2)) * bit
        bit *= 2
    return index


def layer_kernel(
    heads, group, rounds, depth, span, chunks, exported,
    q_ref, k_ref, v_ref, decay_ref, beta_ref, weight_ref, gain_ref, w_hbm_ref,
    o_ref,
    table, rows, local, seen, own, carry, cross, send, recv,
    kept_cols, kept_q, kept_pair, kept_mx,
    normed, parts, kept_own, out_send, out_recv, near_x, near_w, w_ref,
    send_sem, recv_sem, out_send_sem, out_recv_sem,
    x_send_sem, x_recv_sem, ship_send_sem, ship_recv_sem,
    spread_send_sem, spread_recv_sem, core_send_sem, core_recv_sem, w_sem,
):
    step = pl.program_id(0)
    me = lax.axis_index("seq")
    z = lax.axis_index("head")
    tokens = q_ref.shape[0]
    width = q_ref.shape[1] // group
    groups = heads // group
    warm = groups + rounds
    block = tokens // span
    piece = parts.shape[2]
    lane_span = group * width
    seqs = 1 << rounds
    has_left, has_right = z > 0, z < span - 1
    at_end = (z == 0) | (z == span - 1)
    near_low, near_high = z == 1, z == span - 2
    near_end = near_low | near_high
    end_peer = jnp.where(z == 0, 1, span - 2)

    share = near_w.shape[0] // seqs
    mine_at = pl.multiple_of(((me % 2) * (seqs // 2) + me // 2) * share, share)
    core_at = pl.multiple_of((me % 2) * (seqs // 2) * share, share)

    def ship(h):
        at = (pl.ds(mine_at, share), pl.ds(pl.multiple_of(h * piece, piece), piece))
        return pltpu.make_async_remote_copy(
            src_ref=w_hbm_ref.at[at], dst_ref=near_w.at[at],
            send_sem=ship_send_sem.at[h], recv_sem=ship_recv_sem.at[h],
            device_id={"head": end_peer}, device_id_type=MESH,
        )

    def spread(j, h):
        at = (pl.ds(mine_at, share), pl.ds(pl.multiple_of(h * piece, piece), piece))
        return pltpu.make_async_remote_copy(
            src_ref=near_w.at[at], dst_ref=near_w.at[at],
            send_sem=spread_send_sem.at[j - 1, h], recv_sem=spread_recv_sem.at[j - 1, h],
            device_id={"seq": flip(me, 2 * j)}, device_id_type=MESH,
        )

    def core_swap(h):
        at = (pl.ds(core_at, share * seqs // 2), pl.ds(pl.multiple_of(h * piece, piece), piece))
        return pltpu.make_async_remote_copy(
            src_ref=near_w.at[at], dst_ref=near_w.at[at],
            send_sem=core_send_sem.at[h], recv_sem=core_recv_sem.at[h],
            device_id={"seq": flip(me, 1)}, device_id_type=MESH,
        )

    def hand(part, dest):
        at = (
            pl.ds(pl.multiple_of(dest * block, block), block),
            pl.ds(pl.multiple_of(part * lane_span, lane_span), lane_span),
        )
        return pltpu.make_async_remote_copy(
            src_ref=normed.at[at], dst_ref=near_x.at[at],
            send_sem=x_send_sem.at[part, dest], recv_sem=x_recv_sem.at[part, dest],
            device_id={"head": end_peer}, device_id_type=MESH,
        )

    def pass_on(dest, chunk):
        peer = jnp.where(dest > z, z + 1, z - 1)
        slot = jnp.where((dest < z) & (dest == peer), span, dest)
        return pltpu.make_async_remote_copy(
            src_ref=out_send.at[dest, chunk], dst_ref=out_recv.at[slot, chunk],
            send_sem=out_send_sem.at[dest, chunk], recv_sem=out_recv_sem.at[slot, chunk],
            device_id={"head": peer}, device_id_type=MESH,
        )

    def arrival(slot, chunk):
        pltpu.make_async_remote_copy(
            src_ref=out_send.at[0, chunk], dst_ref=out_recv.at[slot, chunk],
            send_sem=out_send_sem.at[0, chunk], recv_sem=out_recv_sem.at[slot, chunk],
            device_id={"head": jnp.where(z == 0, 1, z - 1)}, device_id_type=MESH,
        ).wait_recv()
        return out_recv[slot, chunk].astype(F32)

    def load_weight():
        return pltpu.make_async_copy(w_hbm_ref, w_ref, w_sem)

    def partner(r):
        bit = (me // (1 << r)) % 2
        return me + (1 - 2 * bit) * (1 << r), bit

    def copy(r, part):
        first = 1 if r == rounds - 1 else 0
        return pltpu.make_async_remote_copy(
            src_ref=send.at[r, part, pl.ds(first, 2 - first)],
            dst_ref=recv.at[r, part, pl.ds(first, 2 - first)],
            send_sem=send_sem.at[r, part],
            recv_sem=recv_sem.at[r, part],
            device_id={"seq": partner(r)[0]},
            device_id_type=MESH,
        )

    @pl.when(step == 0)
    def _():
        barrier = pltpu.get_barrier_semaphore()
        peers = [1] + [2 * j for j in range(1, seqs // 2)]
        for mask in peers:
            pl.semaphore_signal(
                barrier, inc=1, device_id={"seq": flip(me, mask)}, device_id_type=MESH
            )

        @pl.when(has_left)
        def _():
            pl.semaphore_signal(barrier, inc=1, device_id={"head": z - 1}, device_id_type=MESH)

        @pl.when(has_right)
        def _():
            pl.semaphore_signal(barrier, inc=1, device_id={"head": z + 1}, device_id_type=MESH)

        neighbours = jnp.where(has_left, 1, 0) + jnp.where(has_right, 1, 0)
        pl.semaphore_wait(barrier, neighbours + len(peers))

        @pl.when(at_end)
        def _():
            for h in range(exported):
                ship(h).start()

        load_weight().start()

        total = decay_ref[...]
        lane = lax.broadcasted_iota(jnp.int32, total.shape, 1)
        inside = total
        shift = 1
        while shift < tokens:
            total = total + jnp.where(lane >= shift, pltpu.roll(total, shift, 1), 0.0)
            if shift < BLK:
                inside = inside + jnp.where(lane % BLK >= shift, pltpu.roll(inside, shift, 1), 0.0)
            shift *= 2
        beta = beta_ref[...]
        grown = jnp.exp(inside)
        gamma = jnp.exp(total)
        table[0] = beta * grown
        table[1] = grown
        table[2] = beta
        table[3] = beta * gamma
        table[4] = jnp.exp(total[:, tokens - 1 :] - total)
        table[5] = gamma
        table[6] = total - inside
        table[7] = total
        rows[...] = jnp.zeros_like(rows)

    def start_spread(h):
        ship(h).wait_recv()
        for j in range(1, seqs // 2):
            spread(j, h).start()

    def start_core_swap(h):
        for j in range(1, seqs // 2):
            spread(j, h).wait_recv()
        core_swap(h).start()

    for h in range(2):
        @pl.when(near_end & (step == 1 + h))
        def _():
            start_spread(h)

        @pl.when(near_end & (step == warm - 2))
        def _():
            start_core_swap(h)

    lo, hi = slice(0, HALF), slice(HALF, 2 * HALF)
    per_half = HALF // BLK

    def front(part, fill=lambda: None):
        keep = part % 2
        row, col = places(HALF, HALF)
        below = row > col
        on_below = row >= col
        work = []
        for u in range(group):
            head = part * group + u
            for i in range(7):
                rows[u, i : i + 1, :] = table[i, pl.ds(head, 1), :]
            for level in range(1 + depth):
                rows[u, 7 + level : 8 + level, :] = weight_ref[level, pl.ds(head, 1), :]
            run_row = table[7, pl.ds(head, 1), :]
            cols = rows[u].T
            end = run_row[:, tokens - 1 :]
            shifts = [
                jnp.exp(jnp.minimum(cols[a * BLK : a * BLK + 1, 6:7] - run_row, 1.0 * BLK))
                for a in range(tokens // BLK)
            ]
            lanes = slice(u * width, (u + 1) * width)
            qn = unit_rows(q_ref[:, lanes].astype(F32))
            kn = unit_rows(k_ref[:, lanes].astype(F32))
            kb = kn.astype(B16)
            kl = (cols[:, 0:1] * kn).astype(B16)
            qm = (cols[:, 1:2] * qn).astype(B16)
            fresh = (cols[:, 2:3] * v_ref[:, lanes].astype(F32)).astype(B16)
            faded = (cols[:, 3:4] * kn).astype(B16)
            tail = (cols[:, 4:5] * kn).astype(B16)
            pair = jnp.concatenate([fresh, faded], -1)
            kept_cols[keep, u] = cols
            kept_q[keep, u] = cols[:, 5:6] * qn
            kept_pair[keep, u] = pair

            def scaled(gram, first, at):
                return jnp.concatenate(
                    [
                        gram[i * BLK : (i + 1) * BLK] * shifts[first + i][:, at]
                        for i in range(per_half)
                    ],
                    0,
                )

            top = mm_t(jnp.concatenate([kl[lo], qm[lo]], 0), kb[lo])
            bottom = mm_t(jnp.concatenate([kl[hi], qm[hi]], 0), kb)
            l00 = jnp.where(below, scaled(top[:HALF], 0, lo), 0.0)
            m00 = jnp.where(on_below, scaled(top[HALF:], 0, lo), 0.0).astype(B16)
            l10 = scaled(bottom[:HALF, lo], per_half, lo).astype(B16)
            l11 = jnp.where(below, scaled(bottom[:HALF, hi], per_half, hi), 0.0)
            m10 = scaled(bottom[HALF:, lo], per_half, lo).astype(B16)
            m11 = jnp.where(on_below, scaled(bottom[HALF:, hi], per_half, hi), 0.0).astype(B16)
            kept_mx[keep, u, 0] = m00
            kept_mx[keep, u, 1] = m11
            kept_mx[keep, u, 2] = m10
            work.append((end, pair, tail, l00, l11, l10))
        inverses = block_inverses([low for item in work for low in item[3:5]], fill)
        x10s = [mm(item[5], inverses[2 * u]).astype(B16) for u, item in enumerate(work)]
        fill()
        x10s = [(-mm(inverses[2 * u + 1], x)).astype(B16) for u, x in enumerate(x10s)]
        fill()
        for u, item in enumerate(work):
            head = part * group + u
            end, pair, tail, _, _, _ = item
            x00, x11, x10 = inverses[2 * u], inverses[2 * u + 1], x10s[u]
            r0 = (mm_tl(tail[lo], x00) + mm_tl(tail[hi], x10)).astype(B16)
            r1 = mm_tl(tail[hi], x11).astype(B16)
            states = mm(jnp.concatenate([r0, r1], 1), pair)
            a, b = places(width, width)
            transit = jnp.where(a == b, jnp.exp(end), 0.0) - states[:, width:]
            own[head, 0] = transit
            own[head, 1] = states[:, :width]
            send[0, part, 0, u] = transit.astype(B16)
            send[0, part, 1, u] = states[:, :width].astype(B16)
            kept_mx[keep, u, 3] = x00
            kept_mx[keep, u, 4] = x11
            kept_mx[keep, u, 5] = x10

    def back(part):
        keep = part % 2
        lane_block = lax.broadcasted_iota(jnp.int32, (BLK, 2 * BLK), 1) // BLK
        for u in range(group):
            head = part * group + u
            cols = kept_cols[keep, u]
            m00, m11, m10, x00, x11, x10 = [kept_mx[keep, u, i] for i in range(6)]
            pair = kept_pair[keep, u]
            fresh, faded = pair[:, :width], pair[:, width:]
            p00 = mm(m00, x00)
            yield
            p11 = mm(m11, x11)
            yield
            p10 = mm(jnp.concatenate([m10, m11], 1), jnp.concatenate([x00, x10], 0)).astype(B16)

            def weighted(p, first, cols=cols):
                out = []
                for i in range(per_half):
                    at = slice((first + i) * BLK, (first + i + 1) * BLK)
                    w = [cols[at, 7 + level : 8 + level] for level in range(3)]
                    tiles = []
                    for t in range(HALF // (2 * BLK)):
                        level = [(i ^ (2 * t + s)).bit_length() for s in range(2)]
                        if level[0] == level[1]:
                            scale = w[level[0]]
                        else:
                            scale = jnp.where(lane_block == 0, w[level[0]], w[level[1]])
                        tiles.append(
                            scale * p[i * BLK : (i + 1) * BLK, t * 2 * BLK : (t + 1) * 2 * BLK]
                        )
                    out.append(jnp.concatenate(tiles, 1))
                return jnp.concatenate(out, 0).astype(B16)

            yield
            both = mm(p10, pair[lo])
            yield
            local[head, lo, :] = mm(weighted(p00, 0), fresh[lo])
            yield
            local[head, hi, :] = (
                mm(weighted(p11, per_half), fresh[hi])
                + cols[hi, 7 + depth : 8 + depth] * both[:, :width]
            )
            yield
            seen[head, lo, :] = (kept_q[keep, u, lo, :] - mm(p00.astype(B16), faded[lo])).astype(B16)
            yield
            seen[head, hi, :] = (
                kept_q[keep, u, hi, :] - both[:, width:] - mm(p11.astype(B16), faded[hi])
            ).astype(B16)

    @pl.when(step == 0)
    def _():
        front(step)
        copy(0, step).start()

    @pl.when((step > 0) & (step < groups))
    def _():
        work = back(step - 1)
        front(step, lambda: next(work, None))
        copy(0, step).start()
        for _ in work:
            pass

    for r in range(rounds):
        part = step - 1 - r

        @pl.when((part >= 0) & (part < groups))
        def _():
            copy(r, part).wait_recv()
            upper = partner(r)[1] == 1
            for u in range(group):
                head = part * group + u
                got_e = recv[r, part, 1, u]
                if r == rounds - 1:
                    kept = carry[head] if r > 0 else None
                    far_state = mm(kept.astype(B16), got_e) if r > 0 else got_e.astype(F32)
                    cross[head, :, r * width : (r + 1) * width] = jnp.where(
                        upper, far_state, 0.0
                    ).astype(B16)
                    continue
                got_t = recv[r, part, 0, u]
                if r == 0:
                    a, b = places(width, width)
                    far_state = got_e.astype(F32)
                    moved = got_t.astype(F32)
                    kept = jnp.where(a == b, 1.0, 0.0)
                else:
                    kept = carry[head]
                    both = mm(kept.astype(B16), jnp.concatenate([got_t, got_e], -1))
                    moved, far_state = both[:, :width], both[:, width:]
                cross[head, :, r * width : (r + 1) * width] = jnp.where(
                    upper, far_state, 0.0
                ).astype(B16)
                carry[head] = jnp.where(upper, moved, kept)
                mine_t, mine_e = own[head, 0], own[head, 1]
                left = jnp.where(upper, mine_t, got_t.astype(F32)).astype(B16)
                right_t = jnp.where(upper, got_t.astype(F32), mine_t).astype(B16)
                right_e = jnp.where(upper, got_e.astype(F32), mine_e).astype(B16)
                later = jnp.where(upper, mine_e, got_e.astype(F32))
                joined = mm(left, jnp.concatenate([right_t, right_e], -1))
                new_t = joined[:, :width]
                new_e = joined[:, width:] + later
                own[head, 0] = new_t
                own[head, 1] = new_e
                send[r + 1, part, 0, u] = new_t.astype(B16)
                send[r + 1, part, 1, u] = new_e.astype(B16)
            if r < rounds - 1:
                copy(r + 1, part).start()

    @pl.when(step == groups)
    def _():
        for _ in back(step - 1):
            pass

    def finish(part):
        for u in range(group):
            head = part * group + u
            for r in range(rounds):
                rows[u, r : 1 + r, :] = weight_ref[1 + depth + r, pl.ds(head, 1), :]
            cols = rows[u].T
            far = mm(seen[head], cross[head])
            total = local[head]
            for r in range(rounds):
                total = total + cols[:, r : 1 + r] * far[:, r * width : (r + 1) * width]
            scaled = total * lax.rsqrt(jnp.mean(total * total, -1, keepdims=True) + 1e-06)
            at = pl.ds(pl.multiple_of(head * width, width), width)
            normed[:, at] = (scaled * gain_ref[:, at]).astype(B16)

        @pl.when(at_end)
        def _():
            for k in range(span - 2):
                hand(part, jnp.where(z == 0, span - 1 - k, k)).start()

        for r in range(rounds):
            copy(r, part).wait_send()

    @pl.when(step == groups)
    def _():
        for part in range(groups - rounds):
            finish(part)

    @pl.when((step >= max(rounds, groups)) & (step < warm))
    def _():
        finish(step - rounds)

    def rows_of(dest):
        return pl.ds(pl.multiple_of(dest * block, block), block)

    def cols_of(chunk):
        return pl.ds(pl.multiple_of(chunk * piece, piece), piece)

    def order(index):
        by_export = (index == 0) | (index % 2 == 1)
        turn = (index + 1) // 2
        return by_export, turn, jnp.where(by_export, turn, exported + turn - 1)

    @pl.when(step == warm)
    def _():
        load_weight().wait()

    @pl.when((step == warm) & at_end)
    def _():
        for part in range(groups):
            hand(part, end_peer).start()

        @pl.loop(exported, chunks)
        def _(chunk):
            parts[0] = mm(normed[...], w_ref[:, cols_of(chunk)])
            for k in range(span - 1):
                dest = jnp.where(z == 0, span - 1 - k, k)
                out_send[dest, chunk] = parts[0, rows_of(dest), :].astype(B16)
                pass_on(dest, chunk).start()
            kept_own[chunk] = parts[0, rows_of(z), :]

        @pl.loop(0, exported)
        def _(chunk):
            kept_own[chunk] = mm(normed[rows_of(z), :], w_ref[:, cols_of(chunk)])

        @pl.loop(0, chunks)
        def _(index):
            chunk = order(index)[2]
            got = arrival(jnp.where(z == 0, span, z), chunk)
            o_ref[:, cols_of(chunk)] = (kept_own[chunk] + got).astype(B16)

    @pl.when((step == warm) & ~at_end)
    def _():
        @pl.loop(0, chunks + 1)
        def _(step_index):
            @pl.when(step_index < chunks)
            def _():
                index = step_index
                slot = index % 2
                by_export, turn, chunk = order(index)

                @pl.when(near_end)
                def _():
                    @pl.when(by_export)
                    def _():
                        core_swap(turn).wait_recv()

                    for k in range(span):
                        dest = jnp.where(near_low, span - 1 - k, k)
                        rows = rows_of(dest)
                        parts[slot, rows, :] = mm(normed[rows, :], w_ref[:, cols_of(chunk)])
                        if k < span - 2:
                            @pl.when(index == 0)
                            def _():
                                for part in range(groups):
                                    hand(part, dest).wait_recv()

                            @pl.when(by_export)
                            def _():
                                parts[slot, rows, :] += mm(
                                    near_x[rows, :], near_w[:, cols_of(turn)]
                                )
                            @pl.when(~by_export)
                            def _():
                                parts[slot, rows, :] += arrival(dest, chunk)

                            out_send[dest, chunk] = parts[slot, rows, :].astype(B16)
                            pass_on(dest, chunk).start()

                    @pl.when(by_export & (turn > 0) & (turn < exported - 1))
                    def _():
                        start_spread(turn + 1)

                    @pl.when(~by_export)
                    def _():
                        start_core_swap(turn + 1)

                if span > 4:
                    @pl.when(~near_end)
                    def _():
                        parts[slot] = mm(normed[...], w_ref[:, cols_of(chunk)])

            @pl.when(step_index > 0)
            def _():
                index = step_index - 1
                slot = index % 2
                by_export, turn, chunk = order(index)

                def onward(dest):
                    out_send[dest, chunk] = (
                        parts[slot, rows_of(dest), :] + arrival(dest, chunk)
                    ).astype(B16)
                    pass_on(dest, chunk).start()

                @pl.when(near_end)
                def _():
                    onward(jnp.where(near_low, 0, span - 1))

                if span > 4:
                    for far in range(span - 1):
                        @pl.when(~near_end & (span - 1 - far > z))
                        def _():
                            onward(span - 1 - far)

                        @pl.when(~near_end & (far < z))
                        def _():
                            onward(far)

                @pl.when(near_end & (index == 0))
                def _():
                    for part in range(groups):
                        hand(part, z).wait_recv()

                @pl.when(near_end & by_export)
                def _():
                    rows = rows_of(z)
                    parts[slot, rows, :] += mm(near_x[rows, :], near_w[:, cols_of(turn)])

                inner = jnp.where(near_low, span, z)
                outer = jnp.where(near_low, z, span)
                parts[slot, rows_of(z), :] += arrival(inner, chunk)

                @pl.when(~(by_export & near_end))
                def _():
                    parts[slot, rows_of(z), :] += arrival(outer, chunk)

                o_ref[:, cols_of(chunk)] = parts[slot, rows_of(z), :].astype(B16)

    @pl.when((step == warm) & at_end)
    def _():
        for h in range(exported):
            ship(h).wait_send()
        for part in range(groups):
            for k in range(span - 1):
                hand(part, jnp.where(z == 0, k + 1, k)).wait_send()

    @pl.when((step == warm) & near_end)
    def _():
        for h in range(exported):
            for j in range(1, seqs // 2):
                spread(j, h).wait_send()
            core_swap(h).wait_send()

    @pl.when(step == warm)
    def _():
        @pl.loop(0, chunks)
        def _(chunk):
            for dest in range(span):
                @pl.when((dest != z) & ~((chunk < exported) & at_end))
                def _():
                    pass_on(dest, chunk).wait_send()


def layer(query, keys, values, log_decay, beta, level_weights, norm_gain, out_weight):
    tokens = query.shape[0]
    heads = log_decay.shape[0]
    inner, columns = out_weight.shape
    width = inner // heads
    levels = level_weights.shape[0]
    seqs, span = lax.axis_size("seq"), lax.axis_size("head")
    rounds = seqs.bit_length() - 1
    depth = levels - 1 - rounds
    group = 2
    groups = heads // group
    warm = groups + rounds
    block = tokens // span
    piece = 512
    chunks = columns // piece
    exported = chunks // 2 + 1

    def head_in(i):
        return (0, jnp.minimum(i, groups - 1))

    token_block = pl.BlockSpec((tokens, group * width), head_in)
    whole2 = pl.BlockSpec((heads, tokens), lambda i: (0, 0))
    dma = pltpu.SemaphoreType.DMA
    return pl.pallas_call(
        functools.partial(layer_kernel, heads, group, rounds, depth, span, chunks, exported),
        grid=(warm + 1,),
        out_shape=jax.ShapeDtypeStruct((block, columns), B16),
        in_specs=[
            token_block, token_block, token_block, whole2, whole2,
            pl.BlockSpec((levels, heads, tokens), lambda i: (0, 0, 0)),
            pl.BlockSpec((1, inner), lambda i: (0, 0)),
            pl.BlockSpec(memory_space=pl.ANY),
        ],
        out_specs=pl.BlockSpec((block, columns), lambda i: (0, 0)),
        scratch_shapes=[
            pltpu.VMEM((8, heads, tokens), F32),
            pltpu.VMEM((group, 16, tokens), F32),
            pltpu.VMEM((heads, tokens, width), F32),
            pltpu.VMEM((heads, tokens, width), B16),
            pltpu.VMEM((heads, 2, width, width), F32),
            pltpu.VMEM((heads, width, width), F32),
            pltpu.VMEM((heads, width, rounds * width), B16),
            pltpu.VMEM((rounds, groups, 2, group, width, width), B16),
            pltpu.VMEM((rounds, groups, 2, group, width, width), B16),
            pltpu.VMEM((2, group, tokens, 16), F32),
            pltpu.VMEM((2, group, tokens, width), F32),
            pltpu.VMEM((2, group, tokens, 2 * width), B16),
            pltpu.VMEM((2, group, 6, HALF, HALF), B16),
            pltpu.VMEM((tokens, inner), B16),
            pltpu.VMEM((2, tokens, piece), F32),
            pltpu.VMEM((chunks, block, piece), F32),
            pltpu.VMEM((span, chunks, block, piece), B16),
            pltpu.VMEM((span + 1, chunks, block, piece), B16),
            pltpu.VMEM((tokens, inner), B16),
            pltpu.VMEM((inner, exported * piece), B16),
            pltpu.VMEM((inner, columns), B16),
            dma((rounds, groups)), dma((rounds, groups)),
            dma((span, chunks)), dma((span + 1, chunks)),
            dma((groups, span)), dma((groups, span)),
            dma((exported,)), dma((exported,)),
            dma((seqs // 2 - 1, exported)), dma((seqs // 2 - 1, exported)),
            dma((exported,)), dma((exported,)), dma,
        ],
        compiler_params=pltpu.CompilerParams(
            collective_id=0, has_side_effects=True, vmem_limit_bytes=60 << 20
        ),
    )(
        query, keys, values, log_decay, beta, level_weights, norm_gain.reshape(1, -1),
        out_weight,
    )


def solution(mesh):
    placed = (
        P("seq", "head"),
        P("seq", "head"),
        P("seq", "head"),
        P("head", "seq"),
        P("head", "seq"),
        P(None, "head", "seq"),
        P("head"),
        P("head", None),
    )
    return jax.shard_map(
        layer, mesh=mesh, in_specs=placed, out_specs=P(("seq", "head"), None), check_vma=False
    )
```

```python
import functools

import jax
import jax.numpy as jnp
from jax import lax
from jax.experimental import pallas as pl
from jax.experimental.pallas import tpu as pltpu
from jax.sharding import PartitionSpec as P

BLK = 64
HALF = 256
MESH = pl.DeviceIdType.MESH
F32 = jnp.float32
B16 = jnp.bfloat16


def mm(left, right):
    return jnp.dot(left, right, preferred_element_type=F32)


def mm_t(left, right):
    return lax.dot_general(left, right, (((1,), (1,)), ((), ())), preferred_element_type=F32)


def mm_tl(left, right):
    return lax.dot_general(left, right, (((0,), (0,)), ((), ())), preferred_element_type=F32)


def unit_rows(matrix):
    return matrix * lax.rsqrt(jnp.sum(matrix * matrix, -1, keepdims=True) + 1e-06)


def places(rows, cols):
    return (
        lax.broadcasted_iota(jnp.int32, (rows, cols), 0),
        lax.broadcasted_iota(jnp.int32, (rows, cols), 1),
    )


def block_inverses(lowers, fill):
    quarter = HALF // 4
    row, lane = places(quarter, HALF)
    blk = lane // quarter
    inside = lane % quarter
    apart = row ^ inside
    zero = jnp.zeros((quarter, HALF), B16)

    def spread_out(c):
        return jnp.concatenate([jnp.where(blk == b, c, zero) for b in range(4)], 0)

    def pick(parts):
        chosen = parts[3]
        for b in (2, 1, 0):
            chosen = jnp.where(blk == b, parts[b], chosen)
        return chosen

    def sub(low, i):
        return low[i * quarter : (i + 1) * quarter]

    eye = jnp.where(row == inside, 1.0, 0.0)
    lows = [pick([sub(low, b) for b in range(4)]) for low in lowers]
    ys = [jnp.where(apart < 16, -low, 0.0) for low in lows]
    yb = [y.astype(B16) for y in ys]
    y2 = [mm(y, spread_out(y)) for y in yb]
    fill()
    y2b = [y.astype(B16) for y in y2]
    y34 = [mm(jnp.concatenate([y, z], 0), spread_out(z)) for y, z in zip(yb, y2b)]
    fill()
    first = [eye + a + b + c[:quarter] for a, b, c in zip(ys, y2, y34)]
    y4b = [c[quarter:].astype(B16) for c in y34]
    y58 = [mm(jnp.concatenate([a.astype(B16), y], 0), spread_out(y)) for a, y in zip(first, y4b)]
    fill()
    second = [a + b[:quarter] for a, b in zip(first, y58)]
    y8b = [b[quarter:].astype(B16) for b in y58]
    xs = [a + mm(a.astype(B16), spread_out(y)) for a, y in zip(second, y8b)]
    fill()
    for size in (16, 32):
        ring = (apart >= size) & (apart < 2 * size)
        xb = [x.astype(B16) for x in xs]
        inner = [
            mm(jnp.where(ring, low, 0.0).astype(B16), spread_out(x)).astype(B16)
            for low, x in zip(lows, xb)
        ]
        fill()
        xs = [x - mm(b, spread_out(t)) for x, b, t in zip(xs, xb, inner)]
        fill()
    even = blk % 2 == 0
    xb = [x.astype(B16) for x in xs]
    ring = [
        jnp.where(blk == 0, sub(low, 1), jnp.where(blk == 2, sub(low, 3), 0.0)).astype(B16)
        for low in lowers
    ]
    inner = [mm(r, spread_out(x)).astype(B16) for r, x in zip(ring, xb)]
    fill()
    below = [
        mm(
            jnp.where(even, zero, x),
            jnp.concatenate([zero, jnp.where(blk == 0, t, zero), zero, jnp.where(blk == 2, t, zero)], 0),
        ).astype(B16)
        for x, t in zip(xb, inner)
    ]
    fill()
    tiles = [
        jnp.concatenate([jnp.where(even, x, zero), jnp.where(even, -b, x)], 0)
        for x, b in zip(xb, below)
    ]
    half = HALF // 2
    inner = [
        mm(low[half:, :half].astype(B16), t[:, :half]).astype(B16) for low, t in zip(lowers, tiles)
    ]
    fill()
    below = [(-mm(t[:, half:], i)).astype(B16) for t, i in zip(tiles, inner)]
    fill()
    empty = jnp.zeros((half, half), B16)
    return [
        jnp.concatenate(
            [
                jnp.concatenate([t[:, :half], empty], 1),
                jnp.concatenate([b, t[:, half:]], 1),
            ],
            0,
        )
        for t, b in zip(tiles, below)
    ]


def flip(index, mask):
    bit = 1
    while bit <= mask:
        if mask & bit:
            index = index + (1 - 2 * ((index // bit) % 2)) * bit
        bit *= 2
    return index


def layer_kernel(
    heads, group, rounds, depth, span, chunks, exported,
    q_ref, k_ref, v_ref, decay_ref, beta_ref, weight_ref, gain_ref, w_hbm_ref,
    o_ref,
    table, rows, local, seen, own, carry, cross, send, recv,
    kept_cols, kept_q, kept_pair, kept_mx,
    normed, parts, kept_own, out_send, out_recv, near_x, near_w, w_ref,
    send_sem, recv_sem, out_send_sem, out_recv_sem,
    x_send_sem, x_recv_sem, ship_send_sem, ship_recv_sem,
    spread_send_sem, spread_recv_sem, core_send_sem, core_recv_sem, w_sem,
):
    step = pl.program_id(0)
    me = lax.axis_index("seq")
    z = lax.axis_index("head")
    tokens = q_ref.shape[0]
    width = q_ref.shape[1] // group
    groups = heads // group
    warm = groups + rounds
    block = tokens // span
    piece = parts.shape[2]
    lane_span = group * width
    seqs = 1 << rounds
    has_left, has_right = z > 0, z < span - 1
    at_end = (z == 0) | (z == span - 1)
    near_low, near_high = z == 1, z == span - 2
    near_end = near_low | near_high
    end_peer = jnp.where(z == 0, 1, span - 2)

    share = near_w.shape[0] // seqs
    mine_at = pl.multiple_of(((me % 2) * (seqs // 2) + me // 2) * share, share)
    core_at = pl.multiple_of((me % 2) * (seqs // 2) * share, share)

    def ship(h):
        at = (pl.ds(mine_at, share), pl.ds(pl.multiple_of(h * piece, piece), piece))
        return pltpu.make_async_remote_copy(
            src_ref=w_hbm_ref.at[at], dst_ref=near_w.at[at],
            send_sem=ship_send_sem.at[h], recv_sem=ship_recv_sem.at[h],
            device_id={"head": end_peer}, device_id_type=MESH,
        )

    def spread(j, h):
        at = (pl.ds(mine_at, share), pl.ds(pl.multiple_of(h * piece, piece), piece))
        return pltpu.make_async_remote_copy(
            src_ref=near_w.at[at], dst_ref=near_w.at[at],
            send_sem=spread_send_sem.at[j - 1, h], recv_sem=spread_recv_sem.at[j - 1, h],
            device_id={"seq": flip(me, 2 * j)}, device_id_type=MESH,
        )

    def core_swap(h):
        at = (pl.ds(core_at, share * seqs // 2), pl.ds(pl.multiple_of(h * piece, piece), piece))
        return pltpu.make_async_remote_copy(
            src_ref=near_w.at[at], dst_ref=near_w.at[at],
            send_sem=core_send_sem.at[h], recv_sem=core_recv_sem.at[h],
            device_id={"seq": flip(me, 1)}, device_id_type=MESH,
        )

    def hand(part, dest):
        at = (
            pl.ds(pl.multiple_of(dest * block, block), block),
            pl.ds(pl.multiple_of(part * lane_span, lane_span), lane_span),
        )
        return pltpu.make_async_remote_copy(
            src_ref=normed.at[at], dst_ref=near_x.at[at],
            send_sem=x_send_sem.at[part, dest], recv_sem=x_recv_sem.at[part, dest],
            device_id={"head": end_peer}, device_id_type=MESH,
        )

    def pass_on(dest, chunk):
        peer = jnp.where(dest > z, z + 1, z - 1)
        slot = jnp.where((dest < z) & (dest == peer), span, dest)
        return pltpu.make_async_remote_copy(
            src_ref=out_send.at[dest, chunk], dst_ref=out_recv.at[slot, chunk],
            send_sem=out_send_sem.at[dest, chunk], recv_sem=out_recv_sem.at[slot, chunk],
            device_id={"head": peer}, device_id_type=MESH,
        )

    def arrival(slot, chunk):
        pltpu.make_async_remote_copy(
            src_ref=out_send.at[0, chunk], dst_ref=out_recv.at[slot, chunk],
            send_sem=out_send_sem.at[0, chunk], recv_sem=out_recv_sem.at[slot, chunk],
            device_id={"head": jnp.where(z == 0, 1, z - 1)}, device_id_type=MESH,
        ).wait_recv()
        return out_recv[slot, chunk].astype(F32)

    def load_weight():
        return pltpu.make_async_copy(w_hbm_ref, w_ref, w_sem)

    def partner(r):
        bit = (me // (1 << r)) % 2
        return me + (1 - 2 * bit) * (1 << r), bit

    def copy(r, part):
        first = 1 if r == rounds - 1 else 0
        return pltpu.make_async_remote_copy(
            src_ref=send.at[r, part, pl.ds(first, 2 - first)],
            dst_ref=recv.at[r, part, pl.ds(first, 2 - first)],
            send_sem=send_sem.at[r, part],
            recv_sem=recv_sem.at[r, part],
            device_id={"seq": partner(r)[0]},
            device_id_type=MESH,
        )

    @pl.when(step == 0)
    def _():
        barrier = pltpu.get_barrier_semaphore()
        peers = [1] + [2 * j for j in range(1, seqs // 2)]
        for mask in peers:
            pl.semaphore_signal(
                barrier, inc=1, device_id={"seq": flip(me, mask)}, device_id_type=MESH
            )

        @pl.when(has_left)
        def _():
            pl.semaphore_signal(barrier, inc=1, device_id={"head": z - 1}, device_id_type=MESH)

        @pl.when(has_right)
        def _():
            pl.semaphore_signal(barrier, inc=1, device_id={"head": z + 1}, device_id_type=MESH)

        neighbours = jnp.where(has_left, 1, 0) + jnp.where(has_right, 1, 0)
        pl.semaphore_wait(barrier, neighbours + len(peers))

        @pl.when(at_end)
        def _():
            for h in range(exported):
                ship(h).start()

        load_weight().start()

        total = decay_ref[...]
        lane = lax.broadcasted_iota(jnp.int32, total.shape, 1)
        inside = total
        shift = 1
        while shift < tokens:
            total = total + jnp.where(lane >= shift, pltpu.roll(total, shift, 1), 0.0)
            if shift < BLK:
                inside = inside + jnp.where(lane % BLK >= shift, pltpu.roll(inside, shift, 1), 0.0)
            shift *= 2
        beta = beta_ref[...]
        grown = jnp.exp(inside)
        gamma = jnp.exp(total)
        table[0] = beta * grown
        table[1] = grown
        table[2] = beta
        table[3] = beta * gamma
        table[4] = jnp.exp(total[:, tokens - 1 :] - total)
        table[5] = gamma
        table[6] = total - inside
        table[7] = total
        rows[...] = jnp.zeros_like(rows)

    def start_spread(h):
        ship(h).wait_recv()
        for j in range(1, seqs // 2):
            spread(j, h).start()

    def start_core_swap(h):
        for j in range(1, seqs // 2):
            spread(j, h).wait_recv()
        core_swap(h).start()

    for h in range(2):
        @pl.when(near_end & (step == 1 + h))
        def _():
            start_spread(h)

        @pl.when(near_end & (step == warm - 2))
        def _():
            start_core_swap(h)

    lo, hi = slice(0, HALF), slice(HALF, 2 * HALF)
    per_half = HALF // BLK

    def front(part, fill=lambda: None):
        keep = part % 2
        row, col = places(HALF, HALF)
        below = row > col
        on_below = row >= col
        work = []
        for u in range(group):
            head = part * group + u
            for i in range(7):
                rows[u, i : i + 1, :] = table[i, pl.ds(head, 1), :]
            for level in range(1 + depth):
                rows[u, 7 + level : 8 + level, :] = weight_ref[level, pl.ds(head, 1), :]
            run_row = table[7, pl.ds(head, 1), :]
            cols = rows[u].T
            end = run_row[:, tokens - 1 :]
            shifts = [
                jnp.exp(jnp.minimum(cols[a * BLK : a * BLK + 1, 6:7] - run_row, 1.0 * BLK))
                for a in range(tokens // BLK)
            ]
            lanes = slice(u * width, (u + 1) * width)
            qn = unit_rows(q_ref[:, lanes].astype(F32))
            kn = unit_rows(k_ref[:, lanes].astype(F32))
            kb = kn.astype(B16)
            kl = (cols[:, 0:1] * kn).astype(B16)
            qm = (cols[:, 1:2] * qn).astype(B16)
            fresh = (cols[:, 2:3] * v_ref[:, lanes].astype(F32)).astype(B16)
            faded = (cols[:, 3:4] * kn).astype(B16)
            tail = (cols[:, 4:5] * kn).astype(B16)
            pair = jnp.concatenate([fresh, faded], -1)
            kept_cols[keep, u] = cols
            kept_q[keep, u] = cols[:, 5:6] * qn
            kept_pair[keep, u] = pair

            def scaled(gram, first, at):
                return jnp.concatenate(
                    [
                        gram[i * BLK : (i + 1) * BLK] * shifts[first + i][:, at]
                        for i in range(per_half)
                    ],
                    0,
                )

            top = mm_t(jnp.concatenate([kl[lo], qm[lo]], 0), kb[lo])
            bottom = mm_t(jnp.concatenate([kl[hi], qm[hi]], 0), kb)
            l00 = jnp.where(below, scaled(top[:HALF], 0, lo), 0.0)
            m00 = jnp.where(on_below, scaled(top[HALF:], 0, lo), 0.0).astype(B16)
            l10 = scaled(bottom[:HALF, lo], per_half, lo).astype(B16)
            l11 = jnp.where(below, scaled(bottom[:HALF, hi], per_half, hi), 0.0)
            m10 = scaled(bottom[HALF:, lo], per_half, lo).astype(B16)
            m11 = jnp.where(on_below, scaled(bottom[HALF:, hi], per_half, hi), 0.0).astype(B16)
            kept_mx[keep, u, 0] = m00
            kept_mx[keep, u, 1] = m11
            kept_mx[keep, u, 2] = m10
            work.append((end, pair, tail, l00, l11, l10))
        inverses = block_inverses([low for item in work for low in item[3:5]], fill)
        x10s = [mm(item[5], inverses[2 * u]).astype(B16) for u, item in enumerate(work)]
        fill()
        x10s = [(-mm(inverses[2 * u + 1], x)).astype(B16) for u, x in enumerate(x10s)]
        fill()
        for u, item in enumerate(work):
            head = part * group + u
            end, pair, tail, _, _, _ = item
            x00, x11, x10 = inverses[2 * u], inverses[2 * u + 1], x10s[u]
            r0 = (mm_tl(tail[lo], x00) + mm_tl(tail[hi], x10)).astype(B16)
            r1 = mm_tl(tail[hi], x11).astype(B16)
            states = mm(jnp.concatenate([r0, r1], 1), pair)
            a, b = places(width, width)
            transit = jnp.where(a == b, jnp.exp(end), 0.0) - states[:, width:]
            own[head, 0] = transit
            own[head, 1] = states[:, :width]
            send[0, part, 0, u] = transit.astype(B16)
            send[0, part, 1, u] = states[:, :width].astype(B16)
            kept_mx[keep, u, 3] = x00
            kept_mx[keep, u, 4] = x11
            kept_mx[keep, u, 5] = x10

    def back(part):
        keep = part % 2
        lane_block = lax.broadcasted_iota(jnp.int32, (BLK, 2 * BLK), 1) // BLK
        for u in range(group):
            head = part * group + u
            cols = kept_cols[keep, u]
            m00, m11, m10, x00, x11, x10 = [kept_mx[keep, u, i] for i in range(6)]
            pair = kept_pair[keep, u]
            fresh, faded = pair[:, :width], pair[:, width:]
            p00 = mm(m00, x00)
            yield
            p11 = mm(m11, x11)
            yield
            p10 = mm(jnp.concatenate([m10, m11], 1), jnp.concatenate([x00, x10], 0)).astype(B16)

            def weighted(p, first, cols=cols):
                out = []
                for i in range(per_half):
                    at = slice((first + i) * BLK, (first + i + 1) * BLK)
                    w = [cols[at, 7 + level : 8 + level] for level in range(3)]
                    tiles = []
                    for t in range(HALF // (2 * BLK)):
                        level = [(i ^ (2 * t + s)).bit_length() for s in range(2)]
                        if level[0] == level[1]:
                            scale = w[level[0]]
                        else:
                            scale = jnp.where(lane_block == 0, w[level[0]], w[level[1]])
                        tiles.append(
                            scale * p[i * BLK : (i + 1) * BLK, t * 2 * BLK : (t + 1) * 2 * BLK]
                        )
                    out.append(jnp.concatenate(tiles, 1))
                return jnp.concatenate(out, 0).astype(B16)

            yield
            both = mm(p10, pair[lo])
            yield
            local[head, lo, :] = mm(weighted(p00, 0), fresh[lo])
            yield
            local[head, hi, :] = (
                mm(weighted(p11, per_half), fresh[hi])
                + cols[hi, 7 + depth : 8 + depth] * both[:, :width]
            )
            yield
            seen[head, lo, :] = (kept_q[keep, u, lo, :] - mm(p00.astype(B16), faded[lo])).astype(B16)
            yield
            seen[head, hi, :] = (
                kept_q[keep, u, hi, :] - both[:, width:] - mm(p11.astype(B16), faded[hi])
            ).astype(B16)

    @pl.when(step == 0)
    def _():
        front(step)
        copy(0, step).start()

    @pl.when((step > 0) & (step < groups))
    def _():
        work = back(step - 1)
        front(step, lambda: next(work, None))
        copy(0, step).start()
        for _ in work:
            pass

    for r in range(rounds):
        part = step - 1 - r

        @pl.when((part >= 0) & (part < groups))
        def _():
            copy(r, part).wait_recv()
            upper = partner(r)[1] == 1
            for u in range(group):
                head = part * group + u
                got_e = recv[r, part, 1, u]
                if r == rounds - 1:
                    kept = carry[head] if r > 0 else None
                    far_state = mm(kept.astype(B16), got_e) if r > 0 else got_e.astype(F32)
                    cross[head, :, r * width : (r + 1) * width] = jnp.where(
                        upper, far_state, 0.0
                    ).astype(B16)
                    continue
                got_t = recv[r, part, 0, u]
                if r == 0:
                    a, b = places(width, width)
                    far_state = got_e.astype(F32)
                    moved = got_t.astype(F32)
                    kept = jnp.where(a == b, 1.0, 0.0)
                else:
                    kept = carry[head]
                    both = mm(kept.astype(B16), jnp.concatenate([got_t, got_e], -1))
                    moved, far_state = both[:, :width], both[:, width:]
                cross[head, :, r * width : (r + 1) * width] = jnp.where(
                    upper, far_state, 0.0
                ).astype(B16)
                carry[head] = jnp.where(upper, moved, kept)
                mine_t, mine_e = own[head, 0], own[head, 1]
                left = jnp.where(upper, mine_t, got_t.astype(F32)).astype(B16)
                right_t = jnp.where(upper, got_t.astype(F32), mine_t).astype(B16)
                right_e = jnp.where(upper, got_e.astype(F32), mine_e).astype(B16)
                later = jnp.where(upper, mine_e, got_e.astype(F32))
                joined = mm(left, jnp.concatenate([right_t, right_e], -1))
                new_t = joined[:, :width]
                new_e = joined[:, width:] + later
                own[head, 0] = new_t
                own[head, 1] = new_e
                send[r + 1, part, 0, u] = new_t.astype(B16)
                send[r + 1, part, 1, u] = new_e.astype(B16)
            if r < rounds - 1:
                copy(r + 1, part).start()

    @pl.when(step == groups)
    def _():
        for _ in back(step - 1):
            pass

    def finish(part):
        for u in range(group):
            head = part * group + u
            for r in range(rounds):
                rows[u, r : 1 + r, :] = weight_ref[1 + depth + r, pl.ds(head, 1), :]
            cols = rows[u].T
            far = mm(seen[head], cross[head])
            total = local[head]
            for r in range(rounds):
                total = total + cols[:, r : 1 + r] * far[:, r * width : (r + 1) * width]
            scaled = total * lax.rsqrt(jnp.mean(total * total, -1, keepdims=True) + 1e-06)
            at = pl.ds(pl.multiple_of(head * width, width), width)
            normed[:, at] = (scaled * gain_ref[:, at]).astype(B16)

        @pl.when(at_end)
        def _():
            for k in range(span - 2):
                hand(part, jnp.where(z == 0, span - 1 - k, k)).start()

        for r in range(rounds):
            copy(r, part).wait_send()

    @pl.when(step == groups)
    def _():
        for part in range(groups - rounds):
            finish(part)

    @pl.when((step >= max(rounds, groups)) & (step < warm))
    def _():
        finish(step - rounds)

    def rows_of(dest):
        return pl.ds(pl.multiple_of(dest * block, block), block)

    def cols_of(chunk):
        return pl.ds(pl.multiple_of(chunk * piece, piece), piece)

    def order(index):
        by_export = (index == 0) | (index % 2 == 1)
        turn = (index + 1) // 2
        return by_export, turn, jnp.where(by_export, turn, exported + turn - 1)

    @pl.when(step == warm)
    def _():
        load_weight().wait()

    @pl.when((step == warm) & at_end)
    def _():
        @pl.loop(exported, chunks)
        def _(chunk):
            parts[0] = mm(normed[...], w_ref[:, cols_of(chunk)])
            for k in range(span - 1):
                dest = jnp.where(z == 0, span - 1 - k, k)
                out_send[dest, chunk] = parts[0, rows_of(dest), :].astype(B16)
                pass_on(dest, chunk).start()
            kept_own[chunk] = parts[0, rows_of(z), :]

            @pl.when(chunk == exported)
            def _():
                for part in range(groups):
                    hand(part, end_peer).start()

        @pl.loop(0, exported)
        def _(chunk):
            kept_own[chunk] = mm(normed[rows_of(z), :], w_ref[:, cols_of(chunk)])

        @pl.loop(0, chunks)
        def _(index):
            chunk = order(index)[2]
            got = arrival(jnp.where(z == 0, span, z), chunk)
            o_ref[:, cols_of(chunk)] = (kept_own[chunk] + got).astype(B16)

    @pl.when((step == warm) & ~at_end)
    def _():
        lag = 3

        @pl.loop(0, chunks + lag)
        def _(step_index):
            @pl.when(step_index < chunks)
            def _():
                index = step_index
                slot = index % 2
                by_export, turn, chunk = order(index)

                @pl.when(near_end)
                def _():
                    @pl.when(by_export)
                    def _():
                        core_swap(turn).wait_recv()

                    for k in range(span):
                        dest = jnp.where(near_low, span - 1 - k, k)
                        rows = rows_of(dest)
                        parts[slot, rows, :] = mm(normed[rows, :], w_ref[:, cols_of(chunk)])
                        if k < span - 2:
                            @pl.when(index == 0)
                            def _():
                                for part in range(groups):
                                    hand(part, dest).wait_recv()

                            @pl.when(by_export)
                            def _():
                                parts[slot, rows, :] += mm(
                                    near_x[rows, :], near_w[:, cols_of(turn)]
                                )
                            @pl.when(~by_export)
                            def _():
                                parts[slot, rows, :] += arrival(dest, chunk)

                            out_send[dest, chunk] = parts[slot, rows, :].astype(B16)
                            pass_on(dest, chunk).start()

                    @pl.when(by_export & (turn > 0) & (turn < exported - 1))
                    def _():
                        start_spread(turn + 1)

                    @pl.when(~by_export)
                    def _():
                        start_core_swap(turn + 1)

                if span > 4:
                    @pl.when(~near_end)
                    def _():
                        parts[slot] = mm(normed[...], w_ref[:, cols_of(chunk)])

            @pl.when((step_index > 0) & (step_index <= chunks))
            def _():
                index = step_index - 1
                slot = index % 2
                chunk = order(index)[2]
                kept_own[chunk] = parts[slot, rows_of(z), :]

                def onward(dest):
                    out_send[dest, chunk] = (
                        parts[slot, rows_of(dest), :] + arrival(dest, chunk)
                    ).astype(B16)
                    pass_on(dest, chunk).start()

                @pl.when(near_end)
                def _():
                    onward(jnp.where(near_low, 0, span - 1))

                if span > 4:
                    for far in range(span - 1):
                        @pl.when(~near_end & (span - 1 - far > z))
                        def _():
                            onward(span - 1 - far)

                        @pl.when(~near_end & (far < z))
                        def _():
                            onward(far)

            @pl.when(step_index >= lag)
            def _():
                index = step_index - lag
                by_export, turn, chunk = order(index)

                @pl.when(near_end & (index == 0))
                def _():
                    for part in range(groups):
                        hand(part, z).wait_recv()

                @pl.when(near_end & by_export)
                def _():
                    kept_own[chunk] += mm(near_x[rows_of(z), :], near_w[:, cols_of(turn)])

                inner = jnp.where(near_low, span, z)
                outer = jnp.where(near_low, z, span)
                kept_own[chunk] += arrival(inner, chunk)

                @pl.when(~(by_export & near_end))
                def _():
                    kept_own[chunk] += arrival(outer, chunk)

                o_ref[:, cols_of(chunk)] = kept_own[chunk].astype(B16)

    @pl.when((step == warm) & at_end)
    def _():
        for h in range(exported):
            ship(h).wait_send()
        for part in range(groups):
            for k in range(span - 1):
                hand(part, jnp.where(z == 0, k + 1, k)).wait_send()

    @pl.when((step == warm) & near_end)
    def _():
        for h in range(exported):
            for j in range(1, seqs // 2):
                spread(j, h).wait_send()
            core_swap(h).wait_send()

    @pl.when(step == warm)
    def _():
        @pl.loop(0, chunks)
        def _(chunk):
            for dest in range(span):
                @pl.when((dest != z) & ~((chunk < exported) & at_end))
                def _():
                    pass_on(dest, chunk).wait_send()


def layer(query, keys, values, log_decay, beta, level_weights, norm_gain, out_weight):
    tokens = query.shape[0]
    heads = log_decay.shape[0]
    inner, columns = out_weight.shape
    width = inner // heads
    levels = level_weights.shape[0]
    seqs, span = lax.axis_size("seq"), lax.axis_size("head")
    rounds = seqs.bit_length() - 1
    depth = levels - 1 - rounds
    group = 2
    groups = heads // group
    warm = groups + rounds
    block = tokens // span
    piece = 512
    chunks = columns // piece
    exported = chunks // 2 + 1

    def head_in(i):
        return (0, jnp.minimum(i, groups - 1))

    token_block = pl.BlockSpec((tokens, group * width), head_in)
    whole2 = pl.BlockSpec((heads, tokens), lambda i: (0, 0))
    dma = pltpu.SemaphoreType.DMA
    return pl.pallas_call(
        functools.partial(layer_kernel, heads, group, rounds, depth, span, chunks, exported),
        grid=(warm + 1,),
        out_shape=jax.ShapeDtypeStruct((block, columns), B16),
        in_specs=[
            token_block, token_block, token_block, whole2, whole2,
            pl.BlockSpec((levels, heads, tokens), lambda i: (0, 0, 0)),
            pl.BlockSpec((1, inner), lambda i: (0, 0)),
            pl.BlockSpec(memory_space=pl.ANY),
        ],
        out_specs=pl.BlockSpec((block, columns), lambda i: (0, 0)),
        scratch_shapes=[
            pltpu.VMEM((8, heads, tokens), F32),
            pltpu.VMEM((group, 16, tokens), F32),
            pltpu.VMEM((heads, tokens, width), F32),
            pltpu.VMEM((heads, tokens, width), B16),
            pltpu.VMEM((heads, 2, width, width), F32),
            pltpu.VMEM((heads, width, width), F32),
            pltpu.VMEM((heads, width, rounds * width), B16),
            pltpu.VMEM((rounds, groups, 2, group, width, width), B16),
            pltpu.VMEM((rounds, groups, 2, group, width, width), B16),
            pltpu.VMEM((2, group, tokens, 16), F32),
            pltpu.VMEM((2, group, tokens, width), F32),
            pltpu.VMEM((2, group, tokens, 2 * width), B16),
            pltpu.VMEM((2, group, 6, HALF, HALF), B16),
            pltpu.VMEM((tokens, inner), B16),
            pltpu.VMEM((2, tokens, piece), F32),
            pltpu.VMEM((chunks, block, piece), F32),
            pltpu.VMEM((span, chunks, block, piece), B16),
            pltpu.VMEM((span + 1, chunks, block, piece), B16),
            pltpu.VMEM((tokens, inner), B16),
            pltpu.VMEM((inner, exported * piece), B16),
            pltpu.VMEM((inner, columns), B16),
            dma((rounds, groups)), dma((rounds, groups)),
            dma((span, chunks)), dma((span + 1, chunks)),
            dma((groups, span)), dma((groups, span)),
            dma((exported,)), dma((exported,)),
            dma((seqs // 2 - 1, exported)), dma((seqs // 2 - 1, exported)),
            dma((exported,)), dma((exported,)), dma,
        ],
        compiler_params=pltpu.CompilerParams(
            collective_id=0, has_side_effects=True, vmem_limit_bytes=60 << 20
        ),
    )(
        query, keys, values, log_decay, beta, level_weights, norm_gain.reshape(1, -1),
        out_weight,
    )


def solution(mesh):
    placed = (
        P("seq", "head"),
        P("seq", "head"),
        P("seq", "head"),
        P("head", "seq"),
        P("head", "seq"),
        P(None, "head", "seq"),
        P("head"),
        P("head", None),
    )
    return jax.shard_map(
        layer, mesh=mesh, in_specs=placed, out_specs=P(("seq", "head"), None), check_vma=False
    )
```

```python
import functools

import jax
import jax.numpy as jnp
from jax import lax
from jax.experimental import pallas as pl
from jax.experimental.pallas import tpu as pltpu
from jax.sharding import PartitionSpec as P

BLK = 64
HALF = 256
MESH = pl.DeviceIdType.MESH
F32 = jnp.float32
B16 = jnp.bfloat16


def mm(left, right):
    return jnp.dot(left, right, preferred_element_type=F32)


def mm_t(left, right):
    return lax.dot_general(left, right, (((1,), (1,)), ((), ())), preferred_element_type=F32)


def mm_tl(left, right):
    return lax.dot_general(left, right, (((0,), (0,)), ((), ())), preferred_element_type=F32)


def unit_rows(matrix):
    return matrix * lax.rsqrt(jnp.sum(matrix * matrix, -1, keepdims=True) + 1e-06)


def places(rows, cols):
    return (
        lax.broadcasted_iota(jnp.int32, (rows, cols), 0),
        lax.broadcasted_iota(jnp.int32, (rows, cols), 1),
    )


def block_inverses(lowers, fill):
    quarter = HALF // 4
    row, lane = places(quarter, HALF)
    blk = lane // quarter
    inside = lane % quarter
    apart = row ^ inside
    zero = jnp.zeros((quarter, HALF), B16)

    def spread_out(c):
        return jnp.concatenate([jnp.where(blk == b, c, zero) for b in range(4)], 0)

    def pick(parts):
        chosen = parts[3]
        for b in (2, 1, 0):
            chosen = jnp.where(blk == b, parts[b], chosen)
        return chosen

    def sub(low, i):
        return low[i * quarter : (i + 1) * quarter]

    eye = jnp.where(row == inside, 1.0, 0.0)
    lows = [pick([sub(low, b) for b in range(4)]) for low in lowers]
    ys = [jnp.where(apart < 16, -low, 0.0) for low in lows]
    yb = [y.astype(B16) for y in ys]
    y2 = [mm(y, spread_out(y)) for y in yb]
    fill()
    y2b = [y.astype(B16) for y in y2]
    y34 = [mm(jnp.concatenate([y, z], 0), spread_out(z)) for y, z in zip(yb, y2b)]
    fill()
    first = [eye + a + b + c[:quarter] for a, b, c in zip(ys, y2, y34)]
    y4b = [c[quarter:].astype(B16) for c in y34]
    y58 = [mm(jnp.concatenate([a.astype(B16), y], 0), spread_out(y)) for a, y in zip(first, y4b)]
    fill()
    second = [a + b[:quarter] for a, b in zip(first, y58)]
    y8b = [b[quarter:].astype(B16) for b in y58]
    xs = [a + mm(a.astype(B16), spread_out(y)) for a, y in zip(second, y8b)]
    fill()
    for size in (16, 32):
        ring = (apart >= size) & (apart < 2 * size)
        xb = [x.astype(B16) for x in xs]
        inner = [
            mm(jnp.where(ring, low, 0.0).astype(B16), spread_out(x)).astype(B16)
            for low, x in zip(lows, xb)
        ]
        fill()
        xs = [x - mm(b, spread_out(t)) for x, b, t in zip(xs, xb, inner)]
        fill()
    even = blk % 2 == 0
    xb = [x.astype(B16) for x in xs]
    ring = [
        jnp.where(blk == 0, sub(low, 1), jnp.where(blk == 2, sub(low, 3), 0.0)).astype(B16)
        for low in lowers
    ]
    inner = [mm(r, spread_out(x)).astype(B16) for r, x in zip(ring, xb)]
    fill()
    below = [
        mm(
            jnp.where(even, zero, x),
            jnp.concatenate([zero, jnp.where(blk == 0, t, zero), zero, jnp.where(blk == 2, t, zero)], 0),
        ).astype(B16)
        for x, t in zip(xb, inner)
    ]
    fill()
    tiles = [
        jnp.concatenate([jnp.where(even, x, zero), jnp.where(even, -b, x)], 0)
        for x, b in zip(xb, below)
    ]
    half = HALF // 2
    inner = [
        mm(low[half:, :half].astype(B16), t[:, :half]).astype(B16) for low, t in zip(lowers, tiles)
    ]
    fill()
    below = [(-mm(t[:, half:], i)).astype(B16) for t, i in zip(tiles, inner)]
    fill()
    empty = jnp.zeros((half, half), B16)
    return [
        jnp.concatenate(
            [
                jnp.concatenate([t[:, :half], empty], 1),
                jnp.concatenate([b, t[:, half:]], 1),
            ],
            0,
        )
        for t, b in zip(tiles, below)
    ]


def flip(index, mask):
    bit = 1
    while bit <= mask:
        if mask & bit:
            index = index + (1 - 2 * ((index // bit) % 2)) * bit
        bit *= 2
    return index


def layer_kernel(
    heads, group, rounds, depth, span, chunks, exported,
    q_ref, k_ref, v_ref, decay_ref, beta_ref, weight_ref, gain_ref, w_hbm_ref,
    o_ref,
    table, rows, local, seen, own, carry, cross, send, recv,
    kept_cols, kept_q, kept_pair, kept_mx,
    normed, parts, kept_own, out_send, out_recv, near_x, near_w, w_ref,
    send_sem, recv_sem, out_send_sem, out_recv_sem,
    x_send_sem, x_recv_sem, ship_send_sem, ship_recv_sem,
    spread_send_sem, spread_recv_sem, core_send_sem, core_recv_sem, w_sem,
):
    step = pl.program_id(0)
    me = lax.axis_index("seq")
    z = lax.axis_index("head")
    tokens = q_ref.shape[0]
    width = q_ref.shape[1] // group
    groups = heads // group
    warm = groups + rounds
    block = tokens // span
    piece = parts.shape[2]
    lane_span = group * width
    seqs = 1 << rounds
    has_left, has_right = z > 0, z < span - 1
    at_end = (z == 0) | (z == span - 1)
    near_low, near_high = z == 1, z == span - 2
    near_end = near_low | near_high
    end_peer = jnp.where(z == 0, 1, span - 2)

    share = near_w.shape[0] // seqs
    mine_at = pl.multiple_of(((me % 2) * (seqs // 2) + me // 2) * share, share)
    core_at = pl.multiple_of((me % 2) * (seqs // 2) * share, share)

    def ship(h):
        at = (pl.ds(mine_at, share), pl.ds(pl.multiple_of(h * piece, piece), piece))
        return pltpu.make_async_remote_copy(
            src_ref=w_hbm_ref.at[at], dst_ref=near_w.at[at],
            send_sem=ship_send_sem.at[h], recv_sem=ship_recv_sem.at[h],
            device_id={"head": end_peer}, device_id_type=MESH,
        )

    def spread(j, h):
        at = (pl.ds(mine_at, share), pl.ds(pl.multiple_of(h * piece, piece), piece))
        return pltpu.make_async_remote_copy(
            src_ref=near_w.at[at], dst_ref=near_w.at[at],
            send_sem=spread_send_sem.at[j - 1, h], recv_sem=spread_recv_sem.at[j - 1, h],
            device_id={"seq": flip(me, 2 * j)}, device_id_type=MESH,
        )

    def core_swap(h):
        at = (pl.ds(core_at, share * seqs // 2), pl.ds(pl.multiple_of(h * piece, piece), piece))
        return pltpu.make_async_remote_copy(
            src_ref=near_w.at[at], dst_ref=near_w.at[at],
            send_sem=core_send_sem.at[h], recv_sem=core_recv_sem.at[h],
            device_id={"seq": flip(me, 1)}, device_id_type=MESH,
        )

    def hand(part, dest):
        at = (
            pl.ds(pl.multiple_of(dest * block, block), block),
            pl.ds(pl.multiple_of(part * lane_span, lane_span), lane_span),
        )
        return pltpu.make_async_remote_copy(
            src_ref=normed.at[at], dst_ref=near_x.at[at],
            send_sem=x_send_sem.at[part, dest], recv_sem=x_recv_sem.at[part, dest],
            device_id={"head": end_peer}, device_id_type=MESH,
        )

    def pass_on(dest, chunk):
        peer = jnp.where(dest > z, z + 1, z - 1)
        slot = jnp.where((dest < z) & (dest == peer), span, dest)
        return pltpu.make_async_remote_copy(
            src_ref=out_send.at[dest, chunk], dst_ref=out_recv.at[slot, chunk],
            send_sem=out_send_sem.at[dest, chunk], recv_sem=out_recv_sem.at[slot, chunk],
            device_id={"head": peer}, device_id_type=MESH,
        )

    def arrival(slot, chunk):
        pltpu.make_async_remote_copy(
            src_ref=out_send.at[0, chunk], dst_ref=out_recv.at[slot, chunk],
            send_sem=out_send_sem.at[0, chunk], recv_sem=out_recv_sem.at[slot, chunk],
            device_id={"head": jnp.where(z == 0, 1, z - 1)}, device_id_type=MESH,
        ).wait_recv()
        return out_recv[slot, chunk].astype(F32)

    def load_weight():
        return pltpu.make_async_copy(w_hbm_ref, w_ref, w_sem)

    def partner(r):
        bit = (me // (1 << r)) % 2
        return me + (1 - 2 * bit) * (1 << r), bit

    def copy(r, part):
        first = 1 if r == rounds - 1 else 0
        return pltpu.make_async_remote_copy(
            src_ref=send.at[r, part, pl.ds(first, 2 - first)],
            dst_ref=recv.at[r, part, pl.ds(first, 2 - first)],
            send_sem=send_sem.at[r, part],
            recv_sem=recv_sem.at[r, part],
            device_id={"seq": partner(r)[0]},
            device_id_type=MESH,
        )

    @pl.when(step == 0)
    def _():
        barrier = pltpu.get_barrier_semaphore()
        peers = [1] + [2 * j for j in range(1, seqs // 2)]
        for mask in peers:
            pl.semaphore_signal(
                barrier, inc=1, device_id={"seq": flip(me, mask)}, device_id_type=MESH
            )

        @pl.when(has_left)
        def _():
            pl.semaphore_signal(barrier, inc=1, device_id={"head": z - 1}, device_id_type=MESH)

        @pl.when(has_right)
        def _():
            pl.semaphore_signal(barrier, inc=1, device_id={"head": z + 1}, device_id_type=MESH)

        neighbours = jnp.where(has_left, 1, 0) + jnp.where(has_right, 1, 0)
        pl.semaphore_wait(barrier, neighbours + len(peers))

        @pl.when(at_end)
        def _():
            for h in range(exported):
                ship(h).start()

        load_weight().start()

        total = decay_ref[...]
        lane = lax.broadcasted_iota(jnp.int32, total.shape, 1)
        inside = total
        shift = 1
        while shift < tokens:
            total = total + jnp.where(lane >= shift, pltpu.roll(total, shift, 1), 0.0)
            if shift < BLK:
                inside = inside + jnp.where(lane % BLK >= shift, pltpu.roll(inside, shift, 1), 0.0)
            shift *= 2
        beta = beta_ref[...]
        grown = jnp.exp(inside)
        gamma = jnp.exp(total)
        table[0] = beta * grown
        table[1] = grown
        table[2] = beta
        table[3] = beta * gamma
        table[4] = jnp.exp(total[:, tokens - 1 :] - total)
        table[5] = gamma
        table[6] = total - inside
        table[7] = total
        rows[...] = jnp.zeros_like(rows)

    def start_spread(h):
        ship(h).wait_recv()
        for j in range(1, seqs // 2):
            spread(j, h).start()

    def start_core_swap(h):
        for j in range(1, seqs // 2):
            spread(j, h).wait_recv()
        core_swap(h).start()

    for h in range(2):
        @pl.when(near_end & (step == 1 + h))
        def _():
            start_spread(h)

        @pl.when(near_end & (step == warm - 2))
        def _():
            start_core_swap(h)

    lo, hi = slice(0, HALF), slice(HALF, 2 * HALF)
    per_half = HALF // BLK

    def front(part, fill=lambda: None):
        keep = part % 2
        row, col = places(HALF, HALF)
        below = row > col
        on_below = row >= col
        work = []
        for u in range(group):
            head = part * group + u
            for i in range(7):
                rows[u, i : i + 1, :] = table[i, pl.ds(head, 1), :]
            for level in range(1 + depth):
                rows[u, 7 + level : 8 + level, :] = weight_ref[level, pl.ds(head, 1), :]
            run_row = table[7, pl.ds(head, 1), :]
            cols = rows[u].T
            end = run_row[:, tokens - 1 :]
            shifts = [
                jnp.exp(jnp.minimum(cols[a * BLK : a * BLK + 1, 6:7] - run_row, 1.0 * BLK))
                for a in range(tokens // BLK)
            ]
            lanes = slice(u * width, (u + 1) * width)
            qn = unit_rows(q_ref[:, lanes].astype(F32))
            kn = unit_rows(k_ref[:, lanes].astype(F32))
            kb = kn.astype(B16)
            kl = (cols[:, 0:1] * kn).astype(B16)
            qm = (cols[:, 1:2] * qn).astype(B16)
            fresh = (cols[:, 2:3] * v_ref[:, lanes].astype(F32)).astype(B16)
            faded = (cols[:, 3:4] * kn).astype(B16)
            tail = (cols[:, 4:5] * kn).astype(B16)
            pair = jnp.concatenate([fresh, faded], -1)
            kept_cols[keep, u] = cols
            kept_q[keep, u] = cols[:, 5:6] * qn
            kept_pair[keep, u] = pair

            def scaled(gram, first, at):
                return jnp.concatenate(
                    [
                        gram[i * BLK : (i + 1) * BLK] * shifts[first + i][:, at]
                        for i in range(per_half)
                    ],
                    0,
                )

            top = mm_t(jnp.concatenate([kl[lo], qm[lo]], 0), kb[lo])
            bottom = mm_t(jnp.concatenate([kl[hi], qm[hi]], 0), kb)
            l00 = jnp.where(below, scaled(top[:HALF], 0, lo), 0.0)
            m00 = jnp.where(on_below, scaled(top[HALF:], 0, lo), 0.0).astype(B16)
            l10 = scaled(bottom[:HALF, lo], per_half, lo).astype(B16)
            l11 = jnp.where(below, scaled(bottom[:HALF, hi], per_half, hi), 0.0)
            m10 = scaled(bottom[HALF:, lo], per_half, lo).astype(B16)
            m11 = jnp.where(on_below, scaled(bottom[HALF:, hi], per_half, hi), 0.0).astype(B16)
            kept_mx[keep, u, 0] = m00
            kept_mx[keep, u, 1] = m11
            kept_mx[keep, u, 2] = m10
            work.append((end, pair, tail, l00, l11, l10))
        inverses = block_inverses([low for item in work for low in item[3:5]], fill)
        x10s = [mm(item[5], inverses[2 * u]).astype(B16) for u, item in enumerate(work)]
        fill()
        x10s = [(-mm(inverses[2 * u + 1], x)).astype(B16) for u, x in enumerate(x10s)]
        fill()
        for u, item in enumerate(work):
            head = part * group + u
            end, pair, tail, _, _, _ = item
            x00, x11, x10 = inverses[2 * u], inverses[2 * u + 1], x10s[u]
            r0 = (mm_tl(tail[lo], x00) + mm_tl(tail[hi], x10)).astype(B16)
            r1 = mm_tl(tail[hi], x11).astype(B16)
            states = mm(jnp.concatenate([r0, r1], 1), pair)
            a, b = places(width, width)
            transit = jnp.where(a == b, jnp.exp(end), 0.0) - states[:, width:]
            own[head, 0] = transit
            own[head, 1] = states[:, :width]
            send[0, part, 0, u] = transit.astype(B16)
            send[0, part, 1, u] = states[:, :width].astype(B16)
            kept_mx[keep, u, 3] = x00
            kept_mx[keep, u, 4] = x11
            kept_mx[keep, u, 5] = x10

    def back(part):
        keep = part % 2
        lane_block = lax.broadcasted_iota(jnp.int32, (BLK, 2 * BLK), 1) // BLK
        for u in range(group):
            head = part * group + u
            cols = kept_cols[keep, u]
            m00, m11, m10, x00, x11, x10 = [kept_mx[keep, u, i] for i in range(6)]
            pair = kept_pair[keep, u]
            fresh, faded = pair[:, :width], pair[:, width:]
            p00 = mm(m00, x00)
            yield
            p11 = mm(m11, x11)
            yield
            p10 = mm(jnp.concatenate([m10, m11], 1), jnp.concatenate([x00, x10], 0)).astype(B16)

            def weighted(p, first, cols=cols):
                out = []
                for i in range(per_half):
                    at = slice((first + i) * BLK, (first + i + 1) * BLK)
                    w = [cols[at, 7 + level : 8 + level] for level in range(3)]
                    tiles = []
                    for t in range(HALF // (2 * BLK)):
                        level = [(i ^ (2 * t + s)).bit_length() for s in range(2)]
                        if level[0] == level[1]:
                            scale = w[level[0]]
                        else:
                            scale = jnp.where(lane_block == 0, w[level[0]], w[level[1]])
                        tiles.append(
                            scale * p[i * BLK : (i + 1) * BLK, t * 2 * BLK : (t + 1) * 2 * BLK]
                        )
                    out.append(jnp.concatenate(tiles, 1))
                return jnp.concatenate(out, 0).astype(B16)

            yield
            both = mm(p10, pair[lo])
            yield
            local[head, lo, :] = mm(weighted(p00, 0), fresh[lo])
            yield
            local[head, hi, :] = (
                mm(weighted(p11, per_half), fresh[hi])
                + cols[hi, 7 + depth : 8 + depth] * both[:, :width]
            )
            yield
            seen[head, lo, :] = (kept_q[keep, u, lo, :] - mm(p00.astype(B16), faded[lo])).astype(B16)
            yield
            seen[head, hi, :] = (
                kept_q[keep, u, hi, :] - both[:, width:] - mm(p11.astype(B16), faded[hi])
            ).astype(B16)

    @pl.when(step == 0)
    def _():
        front(step)
        copy(0, step).start()

    @pl.when((step > 0) & (step < groups))
    def _():
        work = back(step - 1)
        front(step, lambda: next(work, None))
        copy(0, step).start()
        for _ in work:
            pass

    for r in range(rounds):
        part = step - 1 - r

        @pl.when((part >= 0) & (part < groups))
        def _():
            copy(r, part).wait_recv()
            upper = partner(r)[1] == 1
            for u in range(group):
                head = part * group + u
                got_e = recv[r, part, 1, u]
                if r == rounds - 1:
                    kept = carry[head] if r > 0 else None
                    far_state = mm(kept.astype(B16), got_e) if r > 0 else got_e.astype(F32)
                    cross[head, :, r * width : (r + 1) * width] = jnp.where(
                        upper, far_state, 0.0
                    ).astype(B16)
                    continue
                got_t = recv[r, part, 0, u]
                if r == 0:
                    a, b = places(width, width)
                    far_state = got_e.astype(F32)
                    moved = got_t.astype(F32)
                    kept = jnp.where(a == b, 1.0, 0.0)
                else:
                    kept = carry[head]
                    both = mm(kept.astype(B16), jnp.concatenate([got_t, got_e], -1))
                    moved, far_state = both[:, :width], both[:, width:]
                cross[head, :, r * width : (r + 1) * width] = jnp.where(
                    upper, far_state, 0.0
                ).astype(B16)
                carry[head] = jnp.where(upper, moved, kept)
                mine_t, mine_e = own[head, 0], own[head, 1]
                left = jnp.where(upper, mine_t, got_t.astype(F32)).astype(B16)
                right_t = jnp.where(upper, got_t.astype(F32), mine_t).astype(B16)
                right_e = jnp.where(upper, got_e.astype(F32), mine_e).astype(B16)
                later = jnp.where(upper, mine_e, got_e.astype(F32))
                joined = mm(left, jnp.concatenate([right_t, right_e], -1))
                new_t = joined[:, :width]
                new_e = joined[:, width:] + later
                own[head, 0] = new_t
                own[head, 1] = new_e
                send[r + 1, part, 0, u] = new_t.astype(B16)
                send[r + 1, part, 1, u] = new_e.astype(B16)
            if r < rounds - 1:
                copy(r + 1, part).start()

    @pl.when(step == groups)
    def _():
        for _ in back(step - 1):
            pass

    def finish(part):
        for u in range(group):
            head = part * group + u
            for r in range(rounds):
                rows[u, r : 1 + r, :] = weight_ref[1 + depth + r, pl.ds(head, 1), :]
            cols = rows[u].T
            far = mm(seen[head], cross[head])
            total = local[head]
            for r in range(rounds):
                total = total + cols[:, r : 1 + r] * far[:, r * width : (r + 1) * width]
            scaled = total * lax.rsqrt(jnp.mean(total * total, -1, keepdims=True) + 1e-06)
            at = pl.ds(pl.multiple_of(head * width, width), width)
            normed[:, at] = (scaled * gain_ref[:, at]).astype(B16)

        @pl.when(at_end)
        def _():
            for k in range(span - 2):
                hand(part, jnp.where(z == 0, span - 1 - k, k)).start()

        for r in range(rounds):
            copy(r, part).wait_send()

    @pl.when((step >= rounds) & (step < warm))
    def _():
        finish(step - rounds)

    def rows_of(dest):
        return pl.ds(pl.multiple_of(dest * block, block), block)

    def cols_of(chunk):
        return pl.ds(pl.multiple_of(chunk * piece, piece), piece)

    def order(index):
        by_export = (index == 0) | (index % 2 == 1)
        turn = (index + 1) // 2
        return by_export, turn, jnp.where(by_export, turn, exported + turn - 1)

    @pl.when(step == warm)
    def _():
        load_weight().wait()

    @pl.when((step == warm) & at_end)
    def _():
        @pl.loop(exported, chunks)
        def _(chunk):
            parts[0] = mm(normed[...], w_ref[:, cols_of(chunk)])
            for k in range(span - 1):
                dest = jnp.where(z == 0, span - 1 - k, k)
                out_send[dest, chunk] = parts[0, rows_of(dest), :].astype(B16)
                pass_on(dest, chunk).start()
            kept_own[chunk] = parts[0, rows_of(z), :]

            @pl.when(chunk == exported)
            def _():
                for part in range(groups):
                    hand(part, end_peer).start()

        @pl.loop(0, exported)
        def _(chunk):
            kept_own[chunk] = mm(normed[rows_of(z), :], w_ref[:, cols_of(chunk)])

        @pl.loop(0, chunks)
        def _(index):
            chunk = order(index)[2]
            got = arrival(jnp.where(z == 0, span, z), chunk)
            o_ref[:, cols_of(chunk)] = (kept_own[chunk] + got).astype(B16)

    @pl.when((step == warm) & ~at_end)
    def _():
        lag = 3

        @pl.loop(0, chunks + lag)
        def _(step_index):
            @pl.when(step_index < chunks)
            def _():
                index = step_index
                slot = index % 2
                by_export, turn, chunk = order(index)

                @pl.when(near_end)
                def _():
                    @pl.when(by_export)
                    def _():
                        core_swap(turn).wait_recv()

                    for k in range(span):
                        dest = jnp.where(near_low, span - 1 - k, k)
                        rows = rows_of(dest)
                        parts[slot, rows, :] = mm(normed[rows, :], w_ref[:, cols_of(chunk)])
                        if k < span - 2:
                            @pl.when(index == 0)
                            def _():
                                for part in range(groups):
                                    hand(part, dest).wait_recv()

                            @pl.when(by_export)
                            def _():
                                parts[slot, rows, :] += mm(
                                    near_x[rows, :], near_w[:, cols_of(turn)]
                                )
                            @pl.when(~by_export)
                            def _():
                                parts[slot, rows, :] += arrival(dest, chunk)

                            out_send[dest, chunk] = parts[slot, rows, :].astype(B16)
                            pass_on(dest, chunk).start()

                    @pl.when(by_export & (turn > 0) & (turn < exported - 1))
                    def _():
                        start_spread(turn + 1)

                    @pl.when(~by_export)
                    def _():
                        start_core_swap(turn + 1)

                if span > 4:
                    @pl.when(~near_end)
                    def _():
                        parts[slot] = mm(normed[...], w_ref[:, cols_of(chunk)])

            @pl.when((step_index > 0) & (step_index <= chunks))
            def _():
                index = step_index - 1
                slot = index % 2
                chunk = order(index)[2]
                kept_own[chunk] = parts[slot, rows_of(z), :]

                def onward(dest):
                    out_send[dest, chunk] = (
                        parts[slot, rows_of(dest), :] + arrival(dest, chunk)
                    ).astype(B16)
                    pass_on(dest, chunk).start()

                @pl.when(near_end)
                def _():
                    onward(jnp.where(near_low, 0, span - 1))

                if span > 4:
                    for far in range(span - 1):
                        @pl.when(~near_end & (span - 1 - far > z))
                        def _():
                            onward(span - 1 - far)

                        @pl.when(~near_end & (far < z))
                        def _():
                            onward(far)

            @pl.when(step_index >= lag)
            def _():
                index = step_index - lag
                by_export, turn, chunk = order(index)

                @pl.when(near_end & (index == 0))
                def _():
                    for part in range(groups):
                        hand(part, z).wait_recv()

                @pl.when(near_end & by_export)
                def _():
                    kept_own[chunk] += mm(near_x[rows_of(z), :], near_w[:, cols_of(turn)])

                inner = jnp.where(near_low, span, z)
                outer = jnp.where(near_low, z, span)
                kept_own[chunk] += arrival(inner, chunk)

                @pl.when(~(by_export & near_end))
                def _():
                    kept_own[chunk] += arrival(outer, chunk)

                o_ref[:, cols_of(chunk)] = kept_own[chunk].astype(B16)

    @pl.when((step == warm) & at_end)
    def _():
        for h in range(exported):
            ship(h).wait_send()
        for part in range(groups):
            for k in range(span - 1):
                hand(part, jnp.where(z == 0, k + 1, k)).wait_send()

    @pl.when((step == warm) & near_end)
    def _():
        for h in range(exported):
            for j in range(1, seqs // 2):
                spread(j, h).wait_send()
            core_swap(h).wait_send()

    @pl.when(step == warm)
    def _():
        @pl.loop(0, chunks)
        def _(chunk):
            for dest in range(span):
                @pl.when((dest != z) & ~((chunk < exported) & at_end))
                def _():
                    pass_on(dest, chunk).wait_send()


def layer(query, keys, values, log_decay, beta, level_weights, norm_gain, out_weight):
    tokens = query.shape[0]
    heads = log_decay.shape[0]
    inner, columns = out_weight.shape
    width = inner // heads
    levels = level_weights.shape[0]
    seqs, span = lax.axis_size("seq"), lax.axis_size("head")
    rounds = seqs.bit_length() - 1
    depth = levels - 1 - rounds
    group = 2
    groups = heads // group
    warm = groups + rounds
    block = tokens // span
    piece = 512
    chunks = columns // piece
    exported = chunks // 2 + 1

    def head_in(i):
        return (0, jnp.minimum(i, groups - 1))

    token_block = pl.BlockSpec((tokens, group * width), head_in)
    whole2 = pl.BlockSpec((heads, tokens), lambda i: (0, 0))
    dma = pltpu.SemaphoreType.DMA
    return pl.pallas_call(
        functools.partial(layer_kernel, heads, group, rounds, depth, span, chunks, exported),
        grid=(warm + 1,),
        out_shape=jax.ShapeDtypeStruct((block, columns), B16),
        in_specs=[
            token_block, token_block, token_block, whole2, whole2,
            pl.BlockSpec((levels, heads, tokens), lambda i: (0, 0, 0)),
            pl.BlockSpec((1, inner), lambda i: (0, 0)),
            pl.BlockSpec(memory_space=pl.ANY),
        ],
        out_specs=pl.BlockSpec((block, columns), lambda i: (0, 0)),
        scratch_shapes=[
            pltpu.VMEM((8, heads, tokens), F32),
            pltpu.VMEM((group, 16, tokens), F32),
            pltpu.VMEM((heads, tokens, width), F32),
            pltpu.VMEM((heads, tokens, width), B16),
            pltpu.VMEM((heads, 2, width, width), F32),
            pltpu.VMEM((heads, width, width), F32),
            pltpu.VMEM((heads, width, rounds * width), B16),
            pltpu.VMEM((rounds, groups, 2, group, width, width), B16),
            pltpu.VMEM((rounds, groups, 2, group, width, width), B16),
            pltpu.VMEM((2, group, tokens, 16), F32),
            pltpu.VMEM((2, group, tokens, width), F32),
            pltpu.VMEM((2, group, tokens, 2 * width), B16),
            pltpu.VMEM((2, group, 6, HALF, HALF), B16),
            pltpu.VMEM((tokens, inner), B16),
            pltpu.VMEM((2, tokens, piece), F32),
            pltpu.VMEM((chunks, block, piece), F32),
            pltpu.VMEM((span, chunks, block, piece), B16),
            pltpu.VMEM((span + 1, chunks, block, piece), B16),
            pltpu.VMEM((tokens, inner), B16),
            pltpu.VMEM((inner, exported * piece), B16),
            pltpu.VMEM((inner, columns), B16),
            dma((rounds, groups)), dma((rounds, groups)),
            dma((span, chunks)), dma((span + 1, chunks)),
            dma((groups, span)), dma((groups, span)),
            dma((exported,)), dma((exported,)),
            dma((seqs // 2 - 1, exported)), dma((seqs // 2 - 1, exported)),
            dma((exported,)), dma((exported,)), dma,
        ],
        compiler_params=pltpu.CompilerParams(
            collective_id=0, has_side_effects=True, vmem_limit_bytes=60 << 20
        ),
    )(
        query, keys, values, log_decay, beta, level_weights, norm_gain.reshape(1, -1),
        out_weight,
    )


def solution(mesh):
    placed = (
        P("seq", "head"),
        P("seq", "head"),
        P("seq", "head"),
        P("head", "seq"),
        P("head", "seq"),
        P(None, "head", "seq"),
        P("head"),
        P("head", None),
    )
    return jax.shard_map(
        layer, mesh=mesh, in_specs=placed, out_specs=P(("seq", "head"), None), check_vma=False
    )
```

```python
import functools

import jax
import jax.numpy as jnp
from jax import lax
from jax.experimental import pallas as pl
from jax.experimental.pallas import tpu as pltpu
from jax.sharding import PartitionSpec as P

BLK = 64
HALF = 256
MESH = pl.DeviceIdType.MESH
F32 = jnp.float32
B16 = jnp.bfloat16


def mm(left, right):
    return jnp.dot(left, right, preferred_element_type=F32)


def mm_t(left, right):
    return lax.dot_general(left, right, (((1,), (1,)), ((), ())), preferred_element_type=F32)


def mm_tl(left, right):
    return lax.dot_general(left, right, (((0,), (0,)), ((), ())), preferred_element_type=F32)


def unit_rows(matrix):
    return matrix * lax.rsqrt(jnp.sum(matrix * matrix, -1, keepdims=True) + 1e-06)


def places(rows, cols):
    return (
        lax.broadcasted_iota(jnp.int32, (rows, cols), 0),
        lax.broadcasted_iota(jnp.int32, (rows, cols), 1),
    )


def block_inverses(lowers, fill):
    quarter = HALF // 4
    row, lane = places(quarter, HALF)
    blk = lane // quarter
    inside = lane % quarter
    apart = row ^ inside
    zero = jnp.zeros((quarter, HALF), B16)

    def spread_out(c):
        return jnp.concatenate([jnp.where(blk == b, c, zero) for b in range(4)], 0)

    def pick(parts):
        chosen = parts[3]
        for b in (2, 1, 0):
            chosen = jnp.where(blk == b, parts[b], chosen)
        return chosen

    def sub(low, i):
        return low[i * quarter : (i + 1) * quarter]

    eye = jnp.where(row == inside, 1.0, 0.0)
    lows = [pick([sub(low, b) for b in range(4)]) for low in lowers]
    ys = [jnp.where(apart < 16, -low, 0.0) for low in lows]
    yb = [y.astype(B16) for y in ys]
    y2 = [mm(y, spread_out(y)) for y in yb]
    fill()
    y2b = [y.astype(B16) for y in y2]
    y34 = [mm(jnp.concatenate([y, z], 0), spread_out(z)) for y, z in zip(yb, y2b)]
    fill()
    first = [eye + a + b + c[:quarter] for a, b, c in zip(ys, y2, y34)]
    y4b = [c[quarter:].astype(B16) for c in y34]
    y58 = [mm(jnp.concatenate([a.astype(B16), y], 0), spread_out(y)) for a, y in zip(first, y4b)]
    fill()
    second = [a + b[:quarter] for a, b in zip(first, y58)]
    y8b = [b[quarter:].astype(B16) for b in y58]
    xs = [a + mm(a.astype(B16), spread_out(y)) for a, y in zip(second, y8b)]
    fill()
    for size in (16, 32):
        ring = (apart >= size) & (apart < 2 * size)
        xb = [x.astype(B16) for x in xs]
        inner = [
            mm(jnp.where(ring, low, 0.0).astype(B16), spread_out(x)).astype(B16)
            for low, x in zip(lows, xb)
        ]
        fill()
        xs = [x - mm(b, spread_out(t)) for x, b, t in zip(xs, xb, inner)]
        fill()
    even = blk % 2 == 0
    xb = [x.astype(B16) for x in xs]
    ring = [
        jnp.where(blk == 0, sub(low, 1), jnp.where(blk == 2, sub(low, 3), 0.0)).astype(B16)
        for low in lowers
    ]
    inner = [mm(r, spread_out(x)).astype(B16) for r, x in zip(ring, xb)]
    fill()
    below = [
        mm(
            jnp.where(even, zero, x),
            jnp.concatenate([zero, jnp.where(blk == 0, t, zero), zero, jnp.where(blk == 2, t, zero)], 0),
        ).astype(B16)
        for x, t in zip(xb, inner)
    ]
    fill()
    tiles = [
        jnp.concatenate([jnp.where(even, x, zero), jnp.where(even, -b, x)], 0)
        for x, b in zip(xb, below)
    ]
    half = HALF // 2
    inner = [
        mm(low[half:, :half].astype(B16), t[:, :half]).astype(B16) for low, t in zip(lowers, tiles)
    ]
    fill()
    below = [(-mm(t[:, half:], i)).astype(B16) for t, i in zip(tiles, inner)]
    fill()
    empty = jnp.zeros((half, half), B16)
    return [
        jnp.concatenate(
            [
                jnp.concatenate([t[:, :half], empty], 1),
                jnp.concatenate([b, t[:, half:]], 1),
            ],
            0,
        )
        for t, b in zip(tiles, below)
    ]


def flip(index, mask):
    bit = 1
    while bit <= mask:
        if mask & bit:
            index = index + (1 - 2 * ((index // bit) % 2)) * bit
        bit *= 2
    return index


def layer_kernel(
    heads, group, rounds, depth, span, chunks, exported,
    q_ref, k_ref, v_ref, decay_ref, beta_ref, weight_ref, gain_ref, w_hbm_ref,
    o_ref,
    table, rows, local, seen, own, carry, cross, send, recv,
    kept_cols, kept_q, kept_pair, kept_mx,
    normed, parts, kept_own, out_send, out_recv, near_x, near_w, w_ref,
    send_sem, recv_sem, out_send_sem, out_recv_sem,
    x_send_sem, x_recv_sem, ship_send_sem, ship_recv_sem,
    spread_send_sem, spread_recv_sem, core_send_sem, core_recv_sem, w_sem,
):
    step = pl.program_id(0)
    me = lax.axis_index("seq")
    z = lax.axis_index("head")
    tokens = q_ref.shape[0]
    width = q_ref.shape[1] // group
    groups = heads // group
    warm = groups + rounds
    block = tokens // span
    piece = parts.shape[2]
    lane_span = group * width
    seqs = 1 << rounds
    has_left, has_right = z > 0, z < span - 1
    at_end = (z == 0) | (z == span - 1)
    near_low, near_high = z == 1, z == span - 2
    near_end = near_low | near_high
    end_peer = jnp.where(z == 0, 1, span - 2)

    share = near_w.shape[0] // seqs
    mine_at = pl.multiple_of(((me % 2) * (seqs // 2) + me // 2) * share, share)
    core_at = pl.multiple_of((me % 2) * (seqs // 2) * share, share)

    def ship(h):
        at = (pl.ds(mine_at, share), pl.ds(pl.multiple_of(h * piece, piece), piece))
        return pltpu.make_async_remote_copy(
            src_ref=w_hbm_ref.at[at], dst_ref=near_w.at[at],
            send_sem=ship_send_sem.at[h], recv_sem=ship_recv_sem.at[h],
            device_id={"head": end_peer}, device_id_type=MESH,
        )

    def spread(j, h):
        at = (pl.ds(mine_at, share), pl.ds(pl.multiple_of(h * piece, piece), piece))
        return pltpu.make_async_remote_copy(
            src_ref=near_w.at[at], dst_ref=near_w.at[at],
            send_sem=spread_send_sem.at[j - 1, h], recv_sem=spread_recv_sem.at[j - 1, h],
            device_id={"seq": flip(me, 2 * j)}, device_id_type=MESH,
        )

    def core_swap(h):
        at = (pl.ds(core_at, share * seqs // 2), pl.ds(pl.multiple_of(h * piece, piece), piece))
        return pltpu.make_async_remote_copy(
            src_ref=near_w.at[at], dst_ref=near_w.at[at],
            send_sem=core_send_sem.at[h], recv_sem=core_recv_sem.at[h],
            device_id={"seq": flip(me, 1)}, device_id_type=MESH,
        )

    def hand(part, dest):
        at = (
            pl.ds(pl.multiple_of(dest * block, block), block),
            pl.ds(pl.multiple_of(part * lane_span, lane_span), lane_span),
        )
        return pltpu.make_async_remote_copy(
            src_ref=normed.at[at], dst_ref=near_x.at[at],
            send_sem=x_send_sem.at[part, dest], recv_sem=x_recv_sem.at[part, dest],
            device_id={"head": end_peer}, device_id_type=MESH,
        )

    def pass_on(dest, chunk):
        peer = jnp.where(dest > z, z + 1, z - 1)
        slot = jnp.where((dest < z) & (dest == peer), span, dest)
        return pltpu.make_async_remote_copy(
            src_ref=out_send.at[dest, chunk], dst_ref=out_recv.at[slot, chunk],
            send_sem=out_send_sem.at[dest, chunk], recv_sem=out_recv_sem.at[slot, chunk],
            device_id={"head": peer}, device_id_type=MESH,
        )

    def arrival(slot, chunk):
        pltpu.make_async_remote_copy(
            src_ref=out_send.at[0, chunk], dst_ref=out_recv.at[slot, chunk],
            send_sem=out_send_sem.at[0, chunk], recv_sem=out_recv_sem.at[slot, chunk],
            device_id={"head": jnp.where(z == 0, 1, z - 1)}, device_id_type=MESH,
        ).wait_recv()
        return out_recv[slot, chunk].astype(F32)

    def load_weight():
        return pltpu.make_async_copy(w_hbm_ref, w_ref, w_sem)

    def partner(r):
        bit = (me // (1 << r)) % 2
        return me + (1 - 2 * bit) * (1 << r), bit

    def copy(r, part):
        first = 1 if r == rounds - 1 else 0
        return pltpu.make_async_remote_copy(
            src_ref=send.at[r, part, pl.ds(first, 2 - first)],
            dst_ref=recv.at[r, part, pl.ds(first, 2 - first)],
            send_sem=send_sem.at[r, part],
            recv_sem=recv_sem.at[r, part],
            device_id={"seq": partner(r)[0]},
            device_id_type=MESH,
        )

    @pl.when(step == 0)
    def _():
        barrier = pltpu.get_barrier_semaphore()
        peers = [1] + [2 * j for j in range(1, seqs // 2)]
        for mask in peers:
            pl.semaphore_signal(
                barrier, inc=1, device_id={"seq": flip(me, mask)}, device_id_type=MESH
            )

        @pl.when(has_left)
        def _():
            pl.semaphore_signal(barrier, inc=1, device_id={"head": z - 1}, device_id_type=MESH)

        @pl.when(has_right)
        def _():
            pl.semaphore_signal(barrier, inc=1, device_id={"head": z + 1}, device_id_type=MESH)

        neighbours = jnp.where(has_left, 1, 0) + jnp.where(has_right, 1, 0)
        pl.semaphore_wait(barrier, neighbours + len(peers))

        @pl.when(at_end)
        def _():
            for h in range(exported):
                ship(h).start()

        load_weight().start()

        total = decay_ref[...]
        lane = lax.broadcasted_iota(jnp.int32, total.shape, 1)
        inside = total
        shift = 1
        while shift < tokens:
            total = total + jnp.where(lane >= shift, pltpu.roll(total, shift, 1), 0.0)
            if shift < BLK:
                inside = inside + jnp.where(lane % BLK >= shift, pltpu.roll(inside, shift, 1), 0.0)
            shift *= 2
        beta = beta_ref[...]
        grown = jnp.exp(inside)
        gamma = jnp.exp(total)
        table[0] = beta * grown
        table[1] = grown
        table[2] = beta
        table[3] = beta * gamma
        table[4] = jnp.exp(total[:, tokens - 1 :] - total)
        table[5] = gamma
        table[6] = total - inside
        table[7] = total
        rows[...] = jnp.zeros_like(rows)

    def start_spread(h):
        ship(h).wait_recv()
        for j in range(1, seqs // 2):
            spread(j, h).start()

    def start_core_swap(h):
        for j in range(1, seqs // 2):
            spread(j, h).wait_recv()
        core_swap(h).start()

    for h in range(2):
        @pl.when(near_end & (step == 1 + h))
        def _():
            start_spread(h)

        @pl.when(near_end & (step == warm - 2))
        def _():
            start_core_swap(h)

    lo, hi = slice(0, HALF), slice(HALF, 2 * HALF)
    per_half = HALF // BLK

    def front(part, fill=lambda: None):
        keep = part % 2
        row, col = places(HALF, HALF)
        below = row > col
        on_below = row >= col
        work = []
        for u in range(group):
            head = part * group + u
            for i in range(7):
                rows[u, i : i + 1, :] = table[i, pl.ds(head, 1), :]
            for level in range(1 + depth):
                rows[u, 7 + level : 8 + level, :] = weight_ref[level, pl.ds(head, 1), :]
            run_row = table[7, pl.ds(head, 1), :]
            cols = rows[u].T
            end = run_row[:, tokens - 1 :]
            shifts = [
                jnp.exp(jnp.minimum(cols[a * BLK : a * BLK + 1, 6:7] - run_row, 1.0 * BLK))
                for a in range(tokens // BLK)
            ]
            lanes = slice(u * width, (u + 1) * width)
            qn = unit_rows(q_ref[:, lanes].astype(F32))
            kn = unit_rows(k_ref[:, lanes].astype(F32))
            kb = kn.astype(B16)
            kl = (cols[:, 0:1] * kn).astype(B16)
            qm = (cols[:, 1:2] * qn).astype(B16)
            fresh = (cols[:, 2:3] * v_ref[:, lanes].astype(F32)).astype(B16)
            faded = (cols[:, 3:4] * kn).astype(B16)
            tail = (cols[:, 4:5] * kn).astype(B16)
            pair = jnp.concatenate([fresh, faded], -1)
            kept_cols[keep, u] = cols
            kept_q[keep, u] = cols[:, 5:6] * qn
            kept_pair[keep, u] = pair

            def scaled(gram, first, at):
                return jnp.concatenate(
                    [
                        gram[i * BLK : (i + 1) * BLK] * shifts[first + i][:, at]
                        for i in range(per_half)
                    ],
                    0,
                )

            top = mm_t(jnp.concatenate([kl[lo], qm[lo]], 0), kb[lo])
            bottom = mm_t(jnp.concatenate([kl[hi], qm[hi]], 0), kb)
            l00 = jnp.where(below, scaled(top[:HALF], 0, lo), 0.0)
            m00 = jnp.where(on_below, scaled(top[HALF:], 0, lo), 0.0).astype(B16)
            l10 = scaled(bottom[:HALF, lo], per_half, lo).astype(B16)
            l11 = jnp.where(below, scaled(bottom[:HALF, hi], per_half, hi), 0.0)
            m10 = scaled(bottom[HALF:, lo], per_half, lo).astype(B16)
            m11 = jnp.where(on_below, scaled(bottom[HALF:, hi], per_half, hi), 0.0).astype(B16)
            kept_mx[keep, u, 0] = m00
            kept_mx[keep, u, 1] = m11
            kept_mx[keep, u, 2] = m10
            work.append((end, pair, tail, l00, l11, l10))
        inverses = block_inverses([low for item in work for low in item[3:5]], fill)
        x10s = [mm(item[5], inverses[2 * u]).astype(B16) for u, item in enumerate(work)]
        fill()
        x10s = [(-mm(inverses[2 * u + 1], x)).astype(B16) for u, x in enumerate(x10s)]
        fill()
        for u, item in enumerate(work):
            head = part * group + u
            end, pair, tail, _, _, _ = item
            x00, x11, x10 = inverses[2 * u], inverses[2 * u + 1], x10s[u]
            r0 = (mm_tl(tail[lo], x00) + mm_tl(tail[hi], x10)).astype(B16)
            r1 = mm_tl(tail[hi], x11).astype(B16)
            states = mm(jnp.concatenate([r0, r1], 1), pair)
            a, b = places(width, width)
            transit = jnp.where(a == b, jnp.exp(end), 0.0) - states[:, width:]
            own[head, 0] = transit
            own[head, 1] = states[:, :width]
            send[0, part, 0, u] = transit.astype(B16)
            send[0, part, 1, u] = states[:, :width].astype(B16)
            kept_mx[keep, u, 3] = x00
            kept_mx[keep, u, 4] = x11
            kept_mx[keep, u, 5] = x10

    def back(part):
        keep = part % 2
        lane_block = lax.broadcasted_iota(jnp.int32, (BLK, 2 * BLK), 1) // BLK
        for u in range(group):
            head = part * group + u
            cols = kept_cols[keep, u]
            m00, m11, m10, x00, x11, x10 = [kept_mx[keep, u, i] for i in range(6)]
            pair = kept_pair[keep, u]
            fresh, faded = pair[:, :width], pair[:, width:]
            p00 = mm(m00, x00)
            yield
            p11 = mm(m11, x11)
            yield
            p10 = mm(jnp.concatenate([m10, m11], 1), jnp.concatenate([x00, x10], 0)).astype(B16)

            def weighted(p, first, cols=cols):
                out = []
                for i in range(per_half):
                    at = slice((first + i) * BLK, (first + i + 1) * BLK)
                    w = [cols[at, 7 + level : 8 + level] for level in range(3)]
                    tiles = []
                    for t in range(HALF // (2 * BLK)):
                        level = [(i ^ (2 * t + s)).bit_length() for s in range(2)]
                        if level[0] == level[1]:
                            scale = w[level[0]]
                        else:
                            scale = jnp.where(lane_block == 0, w[level[0]], w[level[1]])
                        tiles.append(
                            scale * p[i * BLK : (i + 1) * BLK, t * 2 * BLK : (t + 1) * 2 * BLK]
                        )
                    out.append(jnp.concatenate(tiles, 1))
                return jnp.concatenate(out, 0).astype(B16)

            yield
            both = mm(p10, pair[lo])
            yield
            local[head, lo, :] = mm(weighted(p00, 0), fresh[lo])
            yield
            local[head, hi, :] = (
                mm(weighted(p11, per_half), fresh[hi])
                + cols[hi, 7 + depth : 8 + depth] * both[:, :width]
            )
            yield
            seen[head, lo, :] = (kept_q[keep, u, lo, :] - mm(p00.astype(B16), faded[lo])).astype(B16)
            yield
            seen[head, hi, :] = (
                kept_q[keep, u, hi, :] - both[:, width:] - mm(p11.astype(B16), faded[hi])
            ).astype(B16)

    @pl.when(step == 0)
    def _():
        front(step)
        copy(0, step).start()

    @pl.when((step > 0) & (step < groups))
    def _():
        work = back(step - 1)
        front(step, lambda: next(work, None))
        copy(0, step).start()
        for _ in work:
            pass

    for r in range(rounds):
        part = step - 1 - r

        @pl.when((part >= 0) & (part < groups))
        def _():
            copy(r, part).wait_recv()
            upper = partner(r)[1] == 1
            for u in range(group):
                head = part * group + u
                got_e = recv[r, part, 1, u]
                if r == rounds - 1:
                    kept = carry[head] if r > 0 else None
                    far_state = mm(kept.astype(B16), got_e) if r > 0 else got_e.astype(F32)
                    cross[head, :, r * width : (r + 1) * width] = jnp.where(
                        upper, far_state, 0.0
                    ).astype(B16)
                    continue
                got_t = recv[r, part, 0, u]
                if r == 0:
                    a, b = places(width, width)
                    far_state = got_e.astype(F32)
                    moved = got_t.astype(F32)
                    kept = jnp.where(a == b, 1.0, 0.0)
                else:
                    kept = carry[head]
                    both = mm(kept.astype(B16), jnp.concatenate([got_t, got_e], -1))
                    moved, far_state = both[:, :width], both[:, width:]
                cross[head, :, r * width : (r + 1) * width] = jnp.where(
                    upper, far_state, 0.0
                ).astype(B16)
                carry[head] = jnp.where(upper, moved, kept)
                mine_t, mine_e = own[head, 0], own[head, 1]
                left = jnp.where(upper, mine_t, got_t.astype(F32)).astype(B16)
                right_t = jnp.where(upper, got_t.astype(F32), mine_t).astype(B16)
                right_e = jnp.where(upper, got_e.astype(F32), mine_e).astype(B16)
                later = jnp.where(upper, mine_e, got_e.astype(F32))
                joined = mm(left, jnp.concatenate([right_t, right_e], -1))
                new_t = joined[:, :width]
                new_e = joined[:, width:] + later
                own[head, 0] = new_t
                own[head, 1] = new_e
                send[r + 1, part, 0, u] = new_t.astype(B16)
                send[r + 1, part, 1, u] = new_e.astype(B16)
            if r < rounds - 1:
                copy(r + 1, part).start()

    @pl.when(step == groups)
    def _():
        for _ in back(step - 1):
            pass

    def finish(part):
        for u in range(group):
            head = part * group + u
            for r in range(rounds):
                rows[u, r : 1 + r, :] = weight_ref[1 + depth + r, pl.ds(head, 1), :]
            cols = rows[u].T
            far = mm(seen[head], cross[head])
            total = local[head]
            for r in range(rounds):
                total = total + cols[:, r : 1 + r] * far[:, r * width : (r + 1) * width]
            scaled = total * lax.rsqrt(jnp.mean(total * total, -1, keepdims=True) + 1e-06)
            at = pl.ds(pl.multiple_of(head * width, width), width)
            normed[:, at] = (scaled * gain_ref[:, at]).astype(B16)

        @pl.when(at_end)
        def _():
            for k in range(span - 2):
                hand(part, jnp.where(z == 0, span - 1 - k, k)).start()

        for r in range(rounds):
            copy(r, part).wait_send()

    @pl.when((step >= rounds) & (step < warm))
    def _():
        finish(step - rounds)

    def rows_of(dest):
        return pl.ds(pl.multiple_of(dest * block, block), block)

    def cols_of(chunk):
        return pl.ds(pl.multiple_of(chunk * piece, piece), piece)

    def order(index):
        by_export = (index == 0) | (index % 2 == 1)
        turn = (index + 1) // 2
        return by_export, turn, jnp.where(by_export, turn, exported + turn - 1)

    @pl.when(step == warm)
    def _():
        load_weight().wait()

    @pl.when((step == warm) & at_end)
    def _():
        @pl.loop(exported, chunks)
        def _(chunk):
            parts[0] = mm(normed[...], w_ref[:, cols_of(chunk)])
            for k in range(span - 1):
                dest = jnp.where(z == 0, span - 1 - k, k)
                out_send[dest, chunk] = parts[0, rows_of(dest), :].astype(B16)
                pass_on(dest, chunk).start()
            kept_own[chunk] = parts[0, rows_of(z), :]

            @pl.when(chunk == exported + 1)
            def _():
                for part in range(groups):
                    hand(part, end_peer).start()

        @pl.loop(0, exported)
        def _(chunk):
            kept_own[chunk] = mm(normed[rows_of(z), :], w_ref[:, cols_of(chunk)])

        @pl.loop(0, chunks)
        def _(index):
            chunk = order(index)[2]
            got = arrival(jnp.where(z == 0, span, z), chunk)
            o_ref[:, cols_of(chunk)] = (kept_own[chunk] + got).astype(B16)

    @pl.when((step == warm) & ~at_end)
    def _():
        lag = 5

        @pl.loop(0, chunks + lag)
        def _(step_index):
            @pl.when(step_index < chunks)
            def _():
                index = step_index
                slot = index % 2
                by_export, turn, chunk = order(index)

                @pl.when(near_end)
                def _():
                    @pl.when(by_export)
                    def _():
                        core_swap(turn).wait_recv()

                    for k in range(span):
                        dest = jnp.where(near_low, span - 1 - k, k)
                        rows = rows_of(dest)
                        parts[slot, rows, :] = mm(normed[rows, :], w_ref[:, cols_of(chunk)])
                        if k < span - 2:
                            @pl.when(index == 0)
                            def _():
                                for part in range(groups):
                                    hand(part, dest).wait_recv()

                            @pl.when(by_export)
                            def _():
                                parts[slot, rows, :] += mm(
                                    near_x[rows, :], near_w[:, cols_of(turn)]
                                )
                            @pl.when(~by_export)
                            def _():
                                parts[slot, rows, :] += arrival(dest, chunk)

                            out_send[dest, chunk] = parts[slot, rows, :].astype(B16)
                            pass_on(dest, chunk).start()

                    @pl.when(by_export & (turn > 0) & (turn < exported - 1))
                    def _():
                        start_spread(turn + 1)

                    @pl.when(~by_export)
                    def _():
                        start_core_swap(turn + 1)

                if span > 4:
                    @pl.when(~near_end)
                    def _():
                        parts[slot] = mm(normed[...], w_ref[:, cols_of(chunk)])

            @pl.when((step_index > 0) & (step_index <= chunks))
            def _():
                index = step_index - 1
                slot = index % 2
                chunk = order(index)[2]
                kept_own[chunk] = parts[slot, rows_of(z), :]

                def onward(dest):
                    out_send[dest, chunk] = (
                        parts[slot, rows_of(dest), :] + arrival(dest, chunk)
                    ).astype(B16)
                    pass_on(dest, chunk).start()

                @pl.when(near_end)
                def _():
                    onward(jnp.where(near_low, 0, span - 1))

                if span > 4:
                    for far in range(span - 1):
                        @pl.when(~near_end & (span - 1 - far > z))
                        def _():
                            onward(span - 1 - far)

                        @pl.when(~near_end & (far < z))
                        def _():
                            onward(far)

            @pl.when(step_index >= lag)
            def _():
                index = step_index - lag
                by_export, turn, chunk = order(index)

                @pl.when(near_end & (index == 0))
                def _():
                    for part in range(groups):
                        hand(part, z).wait_recv()

                @pl.when(near_end & by_export)
                def _():
                    kept_own[chunk] += mm(near_x[rows_of(z), :], near_w[:, cols_of(turn)])

                inner = jnp.where(near_low, span, z)
                outer = jnp.where(near_low, z, span)
                kept_own[chunk] += arrival(inner, chunk)

                @pl.when(~(by_export & near_end))
                def _():
                    kept_own[chunk] += arrival(outer, chunk)

                o_ref[:, cols_of(chunk)] = kept_own[chunk].astype(B16)

    @pl.when((step == warm) & at_end)
    def _():
        for h in range(exported):
            ship(h).wait_send()
        for part in range(groups):
            for k in range(span - 1):
                hand(part, jnp.where(z == 0, k + 1, k)).wait_send()

    @pl.when((step == warm) & near_end)
    def _():
        for h in range(exported):
            for j in range(1, seqs // 2):
                spread(j, h).wait_send()
            core_swap(h).wait_send()

    @pl.when(step == warm)
    def _():
        @pl.loop(0, chunks)
        def _(chunk):
            for dest in range(span):
                @pl.when((dest != z) & ~((chunk < exported) & at_end))
                def _():
                    pass_on(dest, chunk).wait_send()


def layer(query, keys, values, log_decay, beta, level_weights, norm_gain, out_weight):
    tokens = query.shape[0]
    heads = log_decay.shape[0]
    inner, columns = out_weight.shape
    width = inner // heads
    levels = level_weights.shape[0]
    seqs, span = lax.axis_size("seq"), lax.axis_size("head")
    rounds = seqs.bit_length() - 1
    depth = levels - 1 - rounds
    group = 2
    groups = heads // group
    warm = groups + rounds
    block = tokens // span
    piece = 512
    chunks = columns // piece
    exported = chunks // 2 + 1

    def head_in(i):
        return (0, jnp.minimum(i, groups - 1))

    token_block = pl.BlockSpec((tokens, group * width), head_in)
    whole2 = pl.BlockSpec((heads, tokens), lambda i: (0, 0))
    dma = pltpu.SemaphoreType.DMA
    return pl.pallas_call(
        functools.partial(layer_kernel, heads, group, rounds, depth, span, chunks, exported),
        grid=(warm + 1,),
        out_shape=jax.ShapeDtypeStruct((block, columns), B16),
        in_specs=[
            token_block, token_block, token_block, whole2, whole2,
            pl.BlockSpec((levels, heads, tokens), lambda i: (0, 0, 0)),
            pl.BlockSpec((1, inner), lambda i: (0, 0)),
            pl.BlockSpec(memory_space=pl.ANY),
        ],
        out_specs=pl.BlockSpec((block, columns), lambda i: (0, 0)),
        scratch_shapes=[
            pltpu.VMEM((8, heads, tokens), F32),
            pltpu.VMEM((group, 16, tokens), F32),
            pltpu.VMEM((heads, tokens, width), F32),
            pltpu.VMEM((heads, tokens, width), B16),
            pltpu.VMEM((heads, 2, width, width), F32),
            pltpu.VMEM((heads, width, width), F32),
            pltpu.VMEM((heads, width, rounds * width), B16),
            pltpu.VMEM((rounds, groups, 2, group, width, width), B16),
            pltpu.VMEM((rounds, groups, 2, group, width, width), B16),
            pltpu.VMEM((2, group, tokens, 16), F32),
            pltpu.VMEM((2, group, tokens, width), F32),
            pltpu.VMEM((2, group, tokens, 2 * width), B16),
            pltpu.VMEM((2, group, 6, HALF, HALF), B16),
            pltpu.VMEM((tokens, inner), B16),
            pltpu.VMEM((2, tokens, piece), F32),
            pltpu.VMEM((chunks, block, piece), F32),
            pltpu.VMEM((span, chunks, block, piece), B16),
            pltpu.VMEM((span + 1, chunks, block, piece), B16),
            pltpu.VMEM((tokens, inner), B16),
            pltpu.VMEM((inner, exported * piece), B16),
            pltpu.VMEM((inner, columns), B16),
            dma((rounds, groups)), dma((rounds, groups)),
            dma((span, chunks)), dma((span + 1, chunks)),
            dma((groups, span)), dma((groups, span)),
            dma((exported,)), dma((exported,)),
            dma((seqs // 2 - 1, exported)), dma((seqs // 2 - 1, exported)),
            dma((exported,)), dma((exported,)), dma,
        ],
        compiler_params=pltpu.CompilerParams(
            collective_id=0, has_side_effects=True, vmem_limit_bytes=60 << 20
        ),
    )(
        query, keys, values, log_decay, beta, level_weights, norm_gain.reshape(1, -1),
        out_weight,
    )


def solution(mesh):
    placed = (
        P("seq", "head"),
        P("seq", "head"),
        P("seq", "head"),
        P("head", "seq"),
        P("head", "seq"),
        P(None, "head", "seq"),
        P("head"),
        P("head", None),
    )
    return jax.shard_map(
        layer, mesh=mesh, in_specs=placed, out_specs=P(("seq", "head"), None), check_vma=False
    )
```
